512 devices in a mesh: expert: 32 (over z, x_lo), fsdp: 16 (over x_hi, y, core).
Axes of the slice: x: 4 (x_hi: 2, x_lo: 2; x = x_hi * 2 + x_lo), y: 4, z: 16, core: 2. Of those that a mesh axis runs over, the one named last changes fastest.
Arguments:
- tokens: bfloat16 [3584, 4096], P(('expert', 'fsdp')), may hold values from -6 to 6
- expert_ids: int32 [3584, 8], P(('expert', 'fsdp')), may hold values from 0 to 31, all different within a row; in each aligned block of 7 rows (0 to 6, 7 to 13, ...) at most 2 rows name the same one
- gate_scores: float32 [3584, 8], P(('expert', 'fsdp')), may hold values from 0.05 to 1
- w_gate: bfloat16 [32, 1536, 4096], P('expert', 'fsdp'), may hold values from -0.09375 to 0.09375
- w_up: bfloat16 [32, 1536, 4096], P('expert', 'fsdp'), may hold values from -0.09375 to 0.09375
- w_down: bfloat16 [32, 1536, 4096], P('expert', None, 'fsdp'), may hold values from -0.15625 to 0.15625
Outputs:
- mixed: bfloat16 [3584, 4096], P(('expert', 'fsdp'))
The draws below stay inside these ranges and needn't reach their ends.
Inputs may be any that keep to these rules, and one draw needn't show every extreme that they name: `expert_ids`: each token names 8 different experts. Within the 7 tokens of one device (aligned blocks of rows) no expert is named more than 2 times, and in every draw some expert is named exactly 2 times in some block.
All inputs are finite; a program needn't handle non-finite values.
Results may differ from the reference program's by a relative error of at most 0.0057.
Values may be sent and summed in bfloat16 or wider, within the bound.
A program may use at most 64 MiB of HBM per device.

```python
import math
import jax
import jax.numpy as jnp
import numpy as np
from jax import lax

D = 4096
FF = 1536
TOP = 8
TOK_DEV = 7
EXPERTS = 32
CAP = 2
TOKENS = 3584


def shard_levels(key, extent, shards, least, largest):
    factor_of, own = 1.0, jax.random.fold_in(key, 6)
    for dim, blocks in shards:
        steps = jnp.exp(jax.random.uniform(jax.random.fold_in(own, dim), (blocks,), jnp.float32, least / len(shards), largest / len(shards)))
        factor_of = factor_of * jnp.repeat(steps, extent[dim] // blocks).reshape([-1 if axis == dim else 1 for axis in range(len(extent))])
    return factor_of


def routed_block(own_key, own, number, rows, number_of, top, most, lean):
    order = jax.random.permutation(own_key, number_of)
    crowded, usual = shares(number_of, rows * top, most, lean, True), shares(number_of, rows * top, most, lean, False)
    places = jnp.arange(number_of)

    def named(lengths, rotation):
        used = int((lengths > 0).sum())
        fixed = max(1, used // 4)
        shifted = fixed + (places - fixed + rotation * (used - fixed)) % max(1, number_of - fixed)
        return jnp.zeros((number_of,), jnp.int32).at[order[jnp.where(places < fixed, places, shifted)]].set(jnp.asarray(lengths, jnp.int32))

    lengths = jnp.where(number % 4 == 0, named(crowded, number // 4), named(usual, number - number // 4 - 1))
    mixed = jax.random.permutation(jax.random.fold_in(own, 3), number_of)
    source_of, taker = mixed[0:number_of // 2 * 2:2], mixed[1:number_of // 2 * 2:2]
    slack = jnp.minimum(lengths[source_of] - 1, most - lengths[taker]) // 2
    slack = jnp.where((source_of == order[0]) | (taker == order[0]) | (lengths[taker] == 0), 0, jnp.maximum(slack, 0))
    shifted = jax.random.randint(jax.random.fold_in(own, 4), (number_of // 2,), 0, 1 << 20) % (slack + 1)
    lengths = lengths.at[source_of].add(-shifted).at[taker].add(shifted)
    members = jnp.searchsorted(jnp.cumsum(lengths), jnp.arange(rows * top), side="right").astype(jnp.int32)
    listing = members.reshape(top, rows).T
    listing = listing[jax.random.permutation(jax.random.fold_in(own, 1), rows)]
    rotation = jax.random.randint(jax.random.fold_in(own, 2), (rows, 1), 0, top)
    return jnp.take_along_axis(listing, (jnp.arange(top)[None, :] + rotation) % top, axis=1)


def shares(amount, total, bound, lean, full):
    weights = [(1 << 20) // math.isqrt(rank ** lean) + 1 for rank in range(1, amount + 1)]
    largest = bound if full else min(bound, max(-(-total // amount), total * weights[0] // sum(weights)))
    least = 1 if total - largest >= amount - 1 else 0
    holding, rest = [largest] + [least] * (amount - 1), total - largest - least * (amount - 1)
    while rest > 0:
        candidates = [i for i in range(1, amount) if holding[i] < largest] or [i for i in range(1, amount) if holding[i] < bound]
        mass, budget = sum([weights[i] for i in candidates]), rest
        for i in candidates:
            extra = min(bound - holding[i], max(1, budget * weights[i] // mass), rest)
            holding[i] = holding[i] + extra
            rest = rest - extra
    return np.array(holding)


def scatter_about(stream_key, extent, width, limit, pieces=(), kind=jnp.bfloat16):
    array = jax.random.normal(stream_key, extent, jnp.float32) * width
    if len(pieces) > 0:
        array = shard_levels(stream_key, extent, pieces, -0.22, 0.18) * array
    return jnp.clip(array, min=-limit, max=limit).astype(kind)


def setup_inputs(seed: int = 0) -> dict:
    keys = jax.random.split(jax.random.key(seed), 7)
    tokens = scatter_about(keys[0], (TOKENS, D), 1.0, 6.0, ((0, 512),))
    expert_ids_keys = jax.random.split(jax.random.fold_in(keys[1], 1), TOKENS // TOK_DEV)
    expert_ids_turns = jax.random.permutation(jax.random.fold_in(keys[1], 3), TOKENS // TOK_DEV)
    expert_ids = jax.vmap(lambda own, number: routed_block(jax.random.fold_in(keys[1], 2), own, number, TOK_DEV, EXPERTS, TOP, CAP, 2))(expert_ids_keys, expert_ids_turns).reshape((TOKENS, TOP))
    gate_scores = jnp.clip(jnp.exp(math.log(1.0) - 2.9957323 * jax.random.uniform(keys[2], (TOKENS, TOP), jnp.float32) ** shard_levels(keys[2], (TOKENS, TOP), ((0, 512),), -0.2, 0.2)), 0.05, 1.0)
    w_gate = scatter_about(keys[3], (EXPERTS, FF, D), D ** -0.5, 0.09375, ((0, 32), (1, 16)))
    w_up = scatter_about(keys[4], (EXPERTS, FF, D), D ** -0.5, 0.09375, ((0, 32), (1, 16)))
    w_down = scatter_about(keys[5], (EXPERTS, FF, D), FF ** -0.5, 0.15625, ((0, 32), (2, 16)))
    return dict(tokens=tokens, expert_ids=expert_ids, gate_scores=gate_scores, w_gate=w_gate, w_up=w_up, w_down=w_down)


def reference(tokens, expert_ids, gate_scores, w_gate, w_up, w_down):
    num_blocks = TOKENS // TOK_DEV
    weights = gate_scores / jnp.sum(gate_scores, axis=1, keepdims=True)
    expert_iota = jnp.arange(EXPERTS, dtype=jnp.int32)
    matches = (expert_ids[:, :, None] == expert_iota[None, None, :]).astype(jnp.int32)
    chosen = jnp.sum(matches, axis=1, dtype=jnp.int32)
    weight_table = jnp.sum(weights[:, :, None] * matches.astype(jnp.float32), axis=1)
    blocked = chosen.reshape(num_blocks, TOK_DEV, EXPERTS)
    ranks = (jnp.cumsum(blocked, axis=1, dtype=jnp.int32) - blocked).reshape(TOKENS, EXPERTS)
    block_index = jnp.arange(TOKENS, dtype=jnp.int32) // TOK_DEV
    slots = jnp.where(chosen > 0, block_index[:, None] * CAP + ranks, num_blocks * CAP).astype(jnp.int32)
    padded = jnp.concatenate([tokens, jnp.zeros((1, D), jnp.bfloat16)], axis=0)
    token_iota = jnp.arange(TOKENS, dtype=jnp.int32)

    def one_expert(running, item):
        gate_mat, up_mat, down_mat, slot_col, weight_col = item
        table = jnp.full((num_blocks * CAP,), TOKENS, jnp.int32).at[slot_col].set(token_iota, mode="drop")
        routed = padded[table]
        gate_act = jnp.dot(routed, gate_mat.T, preferred_element_type=jnp.float32)
        up_act = jnp.dot(routed, up_mat.T, preferred_element_type=jnp.float32)
        hidden = (jax.nn.silu(gate_act) * up_act).astype(jnp.bfloat16)
        expert_out = jnp.dot(hidden, down_mat, preferred_element_type=jnp.float32).astype(jnp.bfloat16)
        weight_rows = jnp.concatenate([weight_col, jnp.zeros((1,), jnp.float32)])[table]
        running = running.at[table].add(weight_rows[:, None] * expert_out.astype(jnp.float32), mode="drop")
        return running, None

    mixed, _ = lax.scan(one_expert, jnp.zeros((TOKENS, D), jnp.float32), (w_gate, w_up, w_down, slots.T, weight_table.T))
    return mixed.astype(jnp.bfloat16)
```

```python
import functools

import jax
import jax.numpy as jnp
from jax import lax
from jax.experimental import pallas as pl
from jax.experimental.pallas import tpu as pltpu
from jax.sharding import PartitionSpec as P

MESH = pl.DeviceIdType.MESH
ANY = pl.BlockSpec(memory_space=pl.ANY)


def offset_of(i, n):
    return n // 2 + ((i % 2) * 2 - 1) * ((i + 1) // 2)


def greet_all(axis, n):
    me = lax.axis_index(axis)
    barrier = pltpu.get_barrier_semaphore()

    def greet(i, carry):
        partner = lax.rem(me + i, n)
        pl.semaphore_signal(barrier, inc=1, device_id={axis: partner}, device_id_type=MESH)
        return carry

    lax.fori_loop(1, n, greet, 0)
    pl.semaphore_wait(barrier, n - 1)


def exchange_kernel(axis, n, x_ref, y_ref, send_sem, recv_sem, own_sem):
    me = lax.axis_index(axis)
    greet_all(axis, n)

    def copy(i, source, target, slot):
        return pltpu.make_async_remote_copy(
            src_ref=x_ref.at[source],
            dst_ref=y_ref.at[slot],
            send_sem=send_sem.at[i],
            recv_sem=recv_sem.at[i],
            device_id={axis: target},
            device_id_type=MESH,
        )

    def send(i, carry):
        partner = lax.rem(me + offset_of(i, n), n)
        copy(i, partner, partner, me).start()
        return carry

    lax.fori_loop(0, n - 1, send, 0)
    own = pltpu.make_async_copy(x_ref.at[me], y_ref.at[me], own_sem)
    own.start()

    def finish(i, carry):
        partner = lax.rem(me + offset_of(i, n), n)
        origin = lax.rem(me - offset_of(i, n) + n, n)
        done = copy(i, partner, partner, origin)
        done.wait_recv()
        done.wait_send()
        return carry

    lax.fori_loop(0, n - 1, finish, 0)
    own.wait()


def exchange(x, axis, n, number):
    return pl.pallas_call(
        functools.partial(exchange_kernel, axis, n),
        out_shape=jax.ShapeDtypeStruct(x.shape, x.dtype),
        in_specs=[ANY],
        out_specs=ANY,
        scratch_shapes=[
            pltpu.SemaphoreType.DMA((n - 1,)),
            pltpu.SemaphoreType.DMA((n - 1,)),
            pltpu.SemaphoreType.DMA,
        ],
        compiler_params=pltpu.CompilerParams(collective_id=number, has_side_effects=True),
    )(x)


def columns_kernel(axis, n, x_ref, y_ref, send_sem, recv_sem, own_sem):
    me = lax.axis_index(axis)
    width = x_ref.shape[2]
    greet_all(axis, n)

    def place(block):
        return y_ref.at[:, pl.ds(pl.multiple_of(block * width, width), width)]

    def copy(i, target, slot):
        return pltpu.make_async_remote_copy(
            src_ref=x_ref.at[target],
            dst_ref=place(slot),
            send_sem=send_sem.at[i],
            recv_sem=recv_sem.at[i],
            device_id={axis: target},
            device_id_type=MESH,
        )

    def send(i, carry):
        copy(i, lax.rem(me + offset_of(i, n), n), me).start()
        return carry

    lax.fori_loop(0, n - 1, send, 0)
    own = pltpu.make_async_copy(x_ref.at[me], place(me), own_sem)
    own.start()

    def finish(i, carry):
        partner = lax.rem(me + offset_of(i, n), n)
        origin = lax.rem(me - offset_of(i, n) + n, n)
        done = copy(i, partner, origin)
        done.wait_recv()
        done.wait_send()
        return carry

    lax.fori_loop(0, n - 1, finish, 0)
    own.wait()


def to_columns(x, axis, n, number):
    return pl.pallas_call(
        functools.partial(columns_kernel, axis, n),
        out_shape=jax.ShapeDtypeStruct((x.shape[1], n * x.shape[2]), x.dtype),
        in_specs=[pl.BlockSpec(memory_space=pltpu.VMEM)],
        out_specs=ANY,
        scratch_shapes=[
            pltpu.SemaphoreType.DMA((n - 1,)),
            pltpu.SemaphoreType.DMA((n - 1,)),
            pltpu.SemaphoreType.DMA,
        ],
        compiler_params=pltpu.CompilerParams(collective_id=number, has_side_effects=True),
    )(x)


def gather_kernel(x_ref, y_ref, send_sem, recv_sem, own_sem):
    me = lax.axis_index("fsdp")
    core, yy, xh = me % 2, (me // 2) % 4, me // 8
    half = x_ref.shape[0] // 2

    def index(h, y, c):
        return (h * 4 + y) * 2 + c

    up, down, far = (yy + 1) % 4, (yy + 3) % 4, (yy + 2) % 4
    other = 1 - xh
    to_up, to_down = index(xh, up, core), index(xh, down, core)
    to_x, to_core = index(other, yy, core), index(xh, yy, 1 - core)

    barrier = pltpu.get_barrier_semaphore()
    for partner in (to_up, to_down, to_x, to_core):
        pl.semaphore_signal(barrier, inc=1, device_id={"fsdp": partner}, device_id_type=MESH)
    pl.semaphore_wait(barrier, 4)

    sent = []

    def place(block, piece):
        return y_ref.at[block, pl.ds(piece * half, half)]

    def send(block, piece, target, own=False):
        copy = pltpu.make_async_remote_copy(
            src_ref=x_ref.at[pl.ds(piece * half, half)] if own else place(block, piece),
            dst_ref=place(block, piece),
            send_sem=send_sem.at[len(sent)],
            recv_sem=recv_sem.at[block, piece],
            device_id={"fsdp": target},
            device_id_type=MESH,
        )
        copy.start()
        sent.append(copy)

    def arrived(block, piece):
        pltpu.make_async_remote_copy(
            src_ref=place(block, piece),
            dst_ref=place(block, piece),
            send_sem=send_sem.at[0],
            recv_sem=recv_sem.at[block, piece],
            device_id={"fsdp": to_core},
            device_id_type=MESH,
        ).wait_recv()

    for piece in (0, 1):
        send(me, piece, to_x, True)
        send(me, piece, to_up, True)
        send(me, 1 - piece, to_down, True)
        send(me, piece, to_core, True)
    own = pltpu.make_async_copy(x_ref, y_ref.at[me], own_sem)
    own.start()

    def ring_first(h):
        block = index(h, down, core)
        arrived(block, 0)
        send(block, 0, to_up)
        send(block, 0, to_core)
        block = index(h, up, core)
        arrived(block, 1)
        send(block, 1, to_down)
        send(block, 1, to_core)

    def ring_rest(h):
        for block, piece in (
            (index(h, down, core), 1),
            (index(h, up, core), 0),
            (index(h, far, core), 0),
            (index(h, far, core), 1),
        ):
            arrived(block, piece)
            send(block, piece, to_core)

    ring_first(xh)
    for piece in (0, 1):
        arrived(to_x, piece)
        send(to_x, piece, to_up)
        send(to_x, piece, to_down)
        send(to_x, piece, to_core)
    ring_rest(xh)
    ring_first(other)
    ring_rest(other)
    for h in (0, 1):
        for y in range(4):
            for piece in (0, 1):
                arrived(index(h, y, 1 - core), piece)
    for copy in sent:
        copy.wait_send()
    own.wait()


def gather(x, number):
    return pl.pallas_call(
        gather_kernel,
        out_shape=jax.ShapeDtypeStruct((16,) + x.shape, x.dtype),
        in_specs=[pl.BlockSpec(memory_space=pltpu.VMEM)],
        out_specs=ANY,
        scratch_shapes=[
            pltpu.SemaphoreType.DMA((30,)),
            pltpu.SemaphoreType.DMA((16, 2)),
            pltpu.SemaphoreType.DMA,
        ],
        compiler_params=pltpu.CompilerParams(collective_id=number, has_side_effects=True),
    )(x)


def on_device(tokens, expert_ids, gate_scores, w_gate, w_up, w_down):
    n_expert = lax.axis_size("expert")
    n_fsdp = lax.axis_size("fsdp")
    local_tok, top_k = expert_ids.shape
    experts = n_expert
    capacity = 2
    width = tokens.shape[1]
    feature_cols = w_down.shape[2]
    weights = gate_scores / jnp.sum(gate_scores, axis=1, keepdims=True)
    expert_iota = lax.broadcasted_iota(jnp.int32, (1, 1, experts), 2)
    matches = (expert_ids[:, :, None] == expert_iota).astype(jnp.int32)
    chosen = jnp.sum(matches, axis=1, dtype=jnp.int32)
    weight_table = jnp.sum(weights[:, :, None] * matches.astype(jnp.float32), axis=1)
    ranks = jnp.cumsum(chosen, axis=0, dtype=jnp.int32) - chosen
    slot_iota = lax.broadcasted_iota(jnp.int32, (1, 1, capacity), 2)
    slot_mask = jnp.logical_and(ranks[:, :, None] == slot_iota, chosen[:, :, None] > 0)
    select_f32 = jnp.transpose(slot_mask.astype(jnp.float32), (1, 2, 0))
    select_bf = select_f32.astype(jnp.bfloat16)
    combine_table = select_f32 * jnp.transpose(weight_table)[:, None, :]
    outgoing = jnp.einsum("ect,td->ecd", select_bf, tokens, preferred_element_type=jnp.float32)
    outgoing = outgoing.astype(jnp.bfloat16)
    arrived = exchange(outgoing, "expert", n_expert, 0)
    routed = gather(arrived.reshape(experts * capacity, width), 1)
    routed = routed.reshape(n_fsdp * experts * capacity, width)
    contract = (((1,), (1,)), ((), ()))
    gate_act = lax.dot_general(w_gate[0], routed, contract, preferred_element_type=jnp.float32)
    up_act = lax.dot_general(w_up[0], routed, contract, preferred_element_type=jnp.float32)
    hidden = (jax.nn.silu(gate_act) * up_act).astype(jnp.bfloat16)
    hidden = gather(hidden, 2)
    hidden = hidden.reshape(w_down.shape[1], hidden.shape[2])
    summed = lax.dot_general(
        hidden, w_down[0], (((0,), (0,)), ((), ())), preferred_element_type=jnp.float32
    )
    expert_out = summed.astype(jnp.bfloat16).reshape(n_fsdp, experts * capacity, feature_cols)
    rows = to_columns(expert_out, "fsdp", n_fsdp, 3)
    returned = exchange(rows.reshape(experts, capacity, width), "expert", n_expert, 4)
    mixed = jnp.einsum(
        "ect,ecd->td", combine_table, returned.astype(jnp.float32), precision=lax.Precision.HIGHEST
    )
    return mixed.astype(jnp.bfloat16)


def solution(mesh):
    placed = (
        P(("expert", "fsdp"), None),
        P(("expert", "fsdp"), None),
        P(("expert", "fsdp"), None),
        P("expert", "fsdp", None),
        P("expert", "fsdp", None),
        P("expert", None, "fsdp"),
    )
    return jax.shard_map(
        on_device,
        mesh=mesh,
        in_specs=placed,
        out_specs=P(("expert", "fsdp"), None),
        check_vma=False,
    )
```

```python
import functools

import jax
import jax.numpy as jnp
from jax import lax
from jax.experimental import pallas as pl
from jax.experimental.pallas import tpu as pltpu
from jax.sharding import PartitionSpec as P

MESH = pl.DeviceIdType.MESH
ANY = pl.BlockSpec(memory_space=pl.ANY)
DMA = pltpu.SemaphoreType.DMA
SLOTS = 2
YS = 4
GROUPS = 4


def fsdp_index(xh, y, core):
    return (xh * YS + y) * 2 + core


def fsdp_place():
    me = lax.axis_index("fsdp")
    return me, me // (2 * YS), (me // 2) % YS, me % 2


def settings(number):
    return pltpu.CompilerParams(
        collective_id=number, has_side_effects=True, vmem_limit_bytes=VMEM
    )


VMEM = 4 * 1024 * 1024


def offset_of(i, n):
    return n // 2 + ((i % 2) * 2 - 1) * ((i + 1) // 2)


def greet_all(axis, n, barrier):
    me = lax.axis_index(axis)

    def greet(i, carry):
        partner = lax.rem(me + i, n)
        pl.semaphore_signal(barrier, inc=1, device_id={axis: partner}, device_id_type=MESH)
        return carry

    lax.fori_loop(1, n, greet, 0)


def quarter_kernel(tok_ref, meta_ref, out_ref, info_ref, send_sem, recv_sem, own_sem):
    me, xh, yy, core = fsdp_place()
    quarter = out_ref.shape[2]
    barrier = pltpu.get_barrier_semaphore()
    for k in range(1, YS):
        pl.semaphore_signal(
            barrier,
            inc=1,
            device_id={"fsdp": fsdp_index(xh, (yy + k) % YS, core)},
            device_id_type=MESH,
        )
    pl.semaphore_wait(barrier, YS - 1)

    def part(y):
        return tok_ref.at[:, pl.ds(pl.multiple_of(y * quarter, quarter), quarter)]

    copies = []
    for k in range(1, YS):
        peer = (yy + k) % YS
        target = {"fsdp": fsdp_index(xh, peer, core)}
        for j, (source, place) in enumerate(
            ((part(peer), out_ref.at[yy]), (meta_ref, info_ref.at[yy]))
        ):
            copy = pltpu.make_async_remote_copy(
                src_ref=source,
                dst_ref=place,
                send_sem=send_sem.at[k - 1, j],
                recv_sem=recv_sem.at[k - 1, j],
                device_id=target,
                device_id_type=MESH,
            )
            copy.start()
            copies.append(copy)
    own = [
        pltpu.make_async_copy(part(yy), out_ref.at[yy], own_sem.at[0]),
        pltpu.make_async_copy(meta_ref, info_ref.at[yy], own_sem.at[1]),
    ]
    for copy in own:
        copy.start()
    for k in range(1, YS):
        origin = (yy + YS - k) % YS
        for j, place in enumerate((out_ref.at[origin], info_ref.at[origin])):
            pltpu.make_async_remote_copy(
                src_ref=place,
                dst_ref=place,
                send_sem=send_sem.at[k - 1, j],
                recv_sem=recv_sem.at[k - 1, j],
                device_id={"fsdp": fsdp_index(xh, origin, core)},
                device_id_type=MESH,
            ).wait_recv()
    for copy in copies:
        copy.wait_send()
    for copy in own:
        copy.wait()


def quarters(tok, meta, number):
    rows, width = tok.shape
    vmem = pl.BlockSpec(memory_space=pltpu.VMEM)
    return pl.pallas_call(
        quarter_kernel,
        out_shape=(
            jax.ShapeDtypeStruct((YS, rows, width // YS), tok.dtype),
            jax.ShapeDtypeStruct((YS,) + meta.shape, meta.dtype),
        ),
        in_specs=[vmem, vmem],
        out_specs=(vmem, vmem),
        scratch_shapes=[DMA((YS - 1, 2)), DMA((YS - 1, 2)), DMA((2,))],
        compiler_params=settings(number),
    )(tok, meta)


def dispatch_kernel(n, x_ref, y_ref, a_send, a_recv, send_sem, recv_sem, own_sem):
    e = lax.axis_index("expert")
    me, xh, yy, core = fsdp_place()
    tall, quarter = x_ref.shape[1], x_ref.shape[2]
    size = n // GROUPS
    other = 1 - xh
    up, down, far = (yy + 1) % YS, (yy + YS - 1) % YS, (yy + 2) % YS
    to_up, to_down = fsdp_index(xh, up, core), fsdp_index(xh, down, core)
    to_x, to_core = fsdp_index(other, yy, core), fsdp_index(xh, yy, 1 - core)

    barrier = pltpu.get_barrier_semaphore()
    for partner in (to_up, to_down, to_x, to_core):
        pl.semaphore_signal(barrier, inc=1, device_id={"fsdp": partner}, device_id_type=MESH)
    greet_all("expert", n, barrier)
    pl.semaphore_wait(barrier, n + 3)

    def place(h, y, c, first, count):
        return y_ref.at[
            h * 2 + c,
            pl.ds(pl.multiple_of(first * tall, tall), count * tall),
            pl.ds(pl.multiple_of(y * quarter, quarter), quarter),
        ]

    def hop(i, target):
        return pltpu.make_async_remote_copy(
            src_ref=x_ref.at[target],
            dst_ref=place(xh, yy, core, i, 1),
            send_sem=a_send.at[i],
            recv_sem=a_recv.at[i],
            device_id={"expert": target},
            device_id_type=MESH,
        )

    def launch(i, carry):
        hop(i, lax.rem(e + offset_of(i, n), n)).start()
        return carry

    def land(i, carry):
        hop(i, lax.rem(e + offset_of(i, n), n)).wait_recv()
        return carry

    def clear(i, carry):
        hop(i, lax.rem(e + offset_of(i, n), n)).wait_send()
        return carry

    lax.fori_loop(0, n - 1, launch, 0)
    own = pltpu.make_async_copy(x_ref.at[e], place(xh, yy, core, n - 1, 1), own_sem)
    own.start()

    sent = []

    def copy_of(h, y, c, g, target, slot):
        block = place(h, y, c, g * size, size)
        return pltpu.make_async_remote_copy(
            src_ref=block,
            dst_ref=block,
            send_sem=send_sem.at[slot],
            recv_sem=recv_sem.at[fsdp_index(h, y, c), g],
            device_id={"fsdp": target},
            device_id_type=MESH,
        )

    def send(h, y, g, *targets):
        for target in targets:
            copy = copy_of(h, y, core, g, target, len(sent))
            copy.start()
            sent.append(copy)

    def arrived(h, y, c, g):
        copy_of(h, y, c, g, to_core, 0).wait_recv()

    def from_expert(g):
        lax.fori_loop(g * size, min((g + 1) * size, n - 1), land, 0)
        if g == GROUPS - 1:
            own.wait()
        send(xh, yy, g, to_x, to_up, to_down, to_core)

    def from_x(g):
        arrived(other, yy, core, g)
        send(other, yy, g, to_up, to_down, to_core)

    def from_ring(h, g):
        for y, onward in ((down, to_up), (up, to_down)):
            arrived(h, y, core, g)
            if (g % 2 == 0) == (onward is to_up):
                send(h, y, g, onward)
            send(h, y, g, to_core)

    def from_far(h, g):
        arrived(h, far, core, g)
        send(h, far, g, to_core)

    for step in range(GROUPS + 2):
        if step < GROUPS:
            from_expert(step)
        if 1 <= step <= GROUPS:
            from_x(step - 1)
            from_ring(xh, step - 1)
        if 2 <= step:
            from_far(xh, step - 2)
            from_ring(other, step - 2)
    for g in range(GROUPS):
        from_far(other, g)
    for g in range(GROUPS):
        for h in (0, 1):
            for y in range(YS):
                arrived(h, y, 1 - core, g)
    lax.fori_loop(0, n - 1, clear, 0)
    for copy in sent:
        copy.wait_send()


def dispatch(x, n, number):
    _, tall, quarter = x.shape
    return pl.pallas_call(
        functools.partial(dispatch_kernel, n),
        out_shape=jax.ShapeDtypeStruct((4, n * tall, YS * quarter), x.dtype),
        in_specs=[ANY],
        out_specs=ANY,
        scratch_shapes=[
            DMA((n - 1,)),
            DMA((n - 1,)),
            DMA((15 * GROUPS,)),
            DMA((16, GROUPS)),
            DMA,
        ],
        compiler_params=settings(number),
    )(x)


def collect_kernel(n, m, x_ref, y_ref, rows, f_send, f_recv, a_send, a_recv, own_sem):
    e = lax.axis_index("expert")
    me = lax.axis_index("fsdp")
    width = x_ref.shape[3]
    size = n // GROUPS
    barrier = pltpu.get_barrier_semaphore()
    greet_all("fsdp", m, barrier)
    greet_all("expert", n, barrier)
    pl.semaphore_wait(barrier, n + m - 2)

    def place(first, count, block):
        return rows.at[
            pl.ds(first, count), :, pl.ds(pl.multiple_of(block * width, width), width)
        ]

    def column(i, target, origin):
        g, k = i // (m - 1), i % (m - 1)
        return pltpu.make_async_remote_copy(
            src_ref=x_ref.at[target, pl.ds(g * size, size)],
            dst_ref=place(g * size, size, origin),
            send_sem=f_send.at[g, k],
            recv_sem=f_recv.at[g, k],
            device_id={"fsdp": target},
            device_id_type=MESH,
        )

    def step_of(i):
        return offset_of(i % (m - 1), m)

    def column_start(i, carry):
        column(i, lax.rem(me + step_of(i), m), me).start()
        return carry

    def column_land(i, carry):
        origin = lax.rem(me - step_of(i) + m, m)
        column(i, origin, origin).wait_recv()
        return carry

    def column_clear(i, carry):
        column(i, lax.rem(me + step_of(i), m), me).wait_send()
        return carry

    own_columns = pltpu.make_async_copy(x_ref.at[me], place(0, n, me), own_sem.at[0])
    own_columns.start()
    lax.fori_loop(0, GROUPS * (m - 1), column_start, 0)
    own_columns.wait()

    def back(i, target, slot):
        return pltpu.make_async_remote_copy(
            src_ref=rows.at[i],
            dst_ref=y_ref.at[slot],
            send_sem=a_send.at[i],
            recv_sem=a_recv.at[i],
            device_id={"expert": target},
            device_id_type=MESH,
        )

    def back_start(i, carry):
        back(i, lax.rem(e - offset_of(i, n) + n, n), e).start()
        return carry

    def back_finish(i, carry):
        origin = lax.rem(e + offset_of(i, n), n)
        done = back(i, origin, origin)
        done.wait_recv()
        done.wait_send()
        return carry

    for g in range(GROUPS):
        lax.fori_loop(g * (m - 1), (g + 1) * (m - 1), column_land, 0)
        lax.fori_loop(g * size, min((g + 1) * size, n - 1), back_start, 0)
    own_rows = pltpu.make_async_copy(rows.at[n - 1], y_ref.at[e], own_sem.at[1])
    own_rows.start()
    lax.fori_loop(0, GROUPS * (m - 1), column_clear, 0)
    lax.fori_loop(0, n - 1, back_finish, 0)
    own_rows.wait()


def collect(x, n, m, number):
    _, _, slots, width = x.shape
    return pl.pallas_call(
        functools.partial(collect_kernel, n, m),
        out_shape=jax.ShapeDtypeStruct((n, slots, m * width), x.dtype),
        in_specs=[ANY],
        out_specs=ANY,
        scratch_shapes=[
            pltpu.VMEM((n, slots, m * width), x.dtype),
            DMA((GROUPS, m - 1)),
            DMA((GROUPS, m - 1)),
            DMA((n - 1,)),
            DMA((n - 1,)),
            DMA((2,)),
        ],
        compiler_params=settings(number),
    )(x)


def gather_kernel(x_ref, y_ref, send_sem, recv_sem, own_sem):
    me = lax.axis_index("fsdp")
    core, yy, xh = me % 2, (me // 2) % 4, me // 8
    half = x_ref.shape[0] // 2

    def index(h, y, c):
        return (h * 4 + y) * 2 + c

    up, down, far = (yy + 1) % 4, (yy + 3) % 4, (yy + 2) % 4
    other = 1 - xh
    to_up, to_down = index(xh, up, core), index(xh, down, core)
    to_x, to_core = index(other, yy, core), index(xh, yy, 1 - core)

    barrier = pltpu.get_barrier_semaphore()
    for partner in (to_up, to_down, to_x, to_core):
        pl.semaphore_signal(barrier, inc=1, device_id={"fsdp": partner}, device_id_type=MESH)
    pl.semaphore_wait(barrier, 4)

    sent = []

    def place(block, piece):
        return y_ref.at[block, pl.ds(piece * half, half)]

    def send(block, piece, target, own=False):
        copy = pltpu.make_async_remote_copy(
            src_ref=x_ref.at[pl.ds(piece * half, half)] if own else place(block, piece),
            dst_ref=place(block, piece),
            send_sem=send_sem.at[len(sent)],
            recv_sem=recv_sem.at[block, piece],
            device_id={"fsdp": target},
            device_id_type=MESH,
        )
        copy.start()
        sent.append(copy)

    def arrived(block, piece):
        pltpu.make_async_remote_copy(
            src_ref=place(block, piece),
            dst_ref=place(block, piece),
            send_sem=send_sem.at[0],
            recv_sem=recv_sem.at[block, piece],
            device_id={"fsdp": to_core},
            device_id_type=MESH,
        ).wait_recv()

    for piece in (0, 1):
        send(me, piece, to_x, True)
        send(me, piece, to_up, True)
        send(me, 1 - piece, to_down, True)
        send(me, piece, to_core, True)
    own = pltpu.make_async_copy(x_ref, y_ref.at[me], own_sem)
    own.start()

    def ring_first(h):
        block = index(h, down, core)
        arrived(block, 0)
        send(block, 0, to_up)
        send(block, 0, to_core)
        block = index(h, up, core)
        arrived(block, 1)
        send(block, 1, to_down)
        send(block, 1, to_core)

    def ring_rest(h):
        for block, piece in (
            (index(h, down, core), 1),
            (index(h, up, core), 0),
            (index(h, far, core), 0),
            (index(h, far, core), 1),
        ):
            arrived(block, piece)
            send(block, piece, to_core)

    ring_first(xh)
    for piece in (0, 1):
        arrived(to_x, piece)
        send(to_x, piece, to_up)
        send(to_x, piece, to_down)
        send(to_x, piece, to_core)
    ring_rest(xh)
    ring_first(other)
    ring_rest(other)
    for h in (0, 1):
        for y in range(4):
            for piece in (0, 1):
                arrived(index(h, y, 1 - core), piece)
    for copy in sent:
        copy.wait_send()
    own.wait()


def gather(x, number):
    return pl.pallas_call(
        gather_kernel,
        out_shape=jax.ShapeDtypeStruct((16,) + x.shape, x.dtype),
        in_specs=[pl.BlockSpec(memory_space=pltpu.VMEM)],
        out_specs=ANY,
        scratch_shapes=[
            pltpu.SemaphoreType.DMA((30,)),
            pltpu.SemaphoreType.DMA((16, 2)),
            pltpu.SemaphoreType.DMA,
        ],
        compiler_params=settings(number),
    )(x)


def route(expert_ids, gate_scores, experts):
    weights = gate_scores / jnp.sum(gate_scores, axis=-1, keepdims=True)
    expert_iota = lax.broadcasted_iota(jnp.int32, (1, 1, experts), 2)
    matches = (expert_ids[:, :, None] == expert_iota).astype(jnp.int32)
    chosen = jnp.sum(matches, axis=1, dtype=jnp.int32)
    weight_table = jnp.sum(weights[:, :, None] * matches.astype(jnp.float32), axis=1)
    return chosen, weight_table


def slots_of(chosen):
    ranks = jnp.cumsum(chosen, axis=-2, dtype=jnp.int32) - chosen
    slot_iota = lax.broadcasted_iota(jnp.int32, (1,) * chosen.ndim + (SLOTS,), chosen.ndim)
    return jnp.logical_and(ranks[..., None] == slot_iota, chosen[..., None] > 0)


def on_device(tokens, expert_ids, gate_scores, w_gate, w_up, w_down):
    n_expert = lax.axis_size("expert")
    n_fsdp = lax.axis_size("fsdp")
    local_tok, top_k = expert_ids.shape
    experts = n_expert
    width = tokens.shape[1]
    feature_cols = w_down.shape[2]
    tall = YS * SLOTS

    chosen, weight_table = route(expert_ids, gate_scores, experts)
    select = jnp.transpose(slots_of(chosen).astype(jnp.float32), (1, 2, 0))
    combine_table = select * jnp.transpose(weight_table)[:, None, :]

    padded = jnp.pad(tokens, ((0, 8 - local_tok), (0, 0)))
    meta = jnp.pad(chosen.astype(jnp.float32), ((0, 8 - local_tok), (0, 128 - experts)))
    tok_quarter, chosen_all = quarters(padded, meta, 0)
    masks = slots_of(chosen_all[:, :, :experts].astype(jnp.int32))
    same = jnp.eye(YS, dtype=jnp.bool_)[None, :, None, :, None]
    table = jnp.transpose(masks, (2, 0, 3, 1))[:, :, :, None, :] & same
    table = table.astype(jnp.bfloat16).reshape(experts * tall, YS * 8)
    outgoing = jnp.dot(
        table, tok_quarter.reshape(YS * 8, width // YS), preferred_element_type=jnp.float32
    )
    outgoing = outgoing.astype(jnp.bfloat16).reshape(experts, tall, width // YS)
    routed = dispatch(outgoing, n_expert, 1).reshape(4 * experts * tall, width)

    contract = (((1,), (1,)), ((), ()))
    gate_act = lax.dot_general(w_gate[0], routed, contract, preferred_element_type=jnp.float32)
    up_act = lax.dot_general(w_up[0], routed, contract, preferred_element_type=jnp.float32)
    hidden = (jax.nn.silu(gate_act) * up_act).astype(jnp.bfloat16)
    hidden = gather(hidden, 2)
    hidden = hidden.reshape(w_down.shape[1], hidden.shape[2])
    summed = lax.dot_general(
        hidden, w_down[0], (((0,), (0,)), ((), ())), preferred_element_type=jnp.float32
    )
    expert_out = summed.astype(jnp.bfloat16).reshape(2, 2, experts, YS, SLOTS, feature_cols)
    expert_out = jnp.transpose(expert_out, (0, 3, 1, 2, 4, 5))
    expert_out = expert_out.reshape(n_fsdp, experts, SLOTS, feature_cols)
    returned = collect(expert_out, n_expert, n_fsdp, 3)
    mixed = jnp.einsum(
        "ect,ecd->td", combine_table, returned.astype(jnp.float32), precision=lax.Precision.HIGHEST
    )
    return mixed.astype(jnp.bfloat16)


def solution(mesh):
    placed = (
        P(("expert", "fsdp"), None),
        P(("expert", "fsdp"), None),
        P(("expert", "fsdp"), None),
        P("expert", "fsdp", None),
        P("expert", "fsdp", None),
        P("expert", None, "fsdp"),
    )
    return jax.shard_map(
        on_device,
        mesh=mesh,
        in_specs=placed,
        out_specs=P(("expert", "fsdp"), None),
        check_vma=False,
    )
```

```python
import functools

import jax
import jax.numpy as jnp
from jax import lax
from jax.experimental import pallas as pl
from jax.experimental.pallas import tpu as pltpu
from jax.sharding import PartitionSpec as P

MESH = pl.DeviceIdType.MESH
ANY = pl.BlockSpec(memory_space=pl.ANY)
DMA = pltpu.SemaphoreType.DMA
SLOTS = 2
YS = 4
GROUPS = 4


def fsdp_index(xh, y, core):
    return (xh * YS + y) * 2 + core


def fsdp_place():
    me = lax.axis_index("fsdp")
    return me, me // (2 * YS), (me // 2) % YS, me % 2


def settings(number):
    return pltpu.CompilerParams(
        collective_id=number, has_side_effects=True, vmem_limit_bytes=VMEM
    )


VMEM = 4 * 1024 * 1024


def offset_of(i, n):
    near = i // 2 + 1
    return near + (i % 2) * (n - 2 * near)


def greet_all(axis, n, barrier):
    me = lax.axis_index(axis)

    def greet(i, carry):
        partner = lax.rem(me + i, n)
        pl.semaphore_signal(barrier, inc=1, device_id={axis: partner}, device_id_type=MESH)
        return carry

    lax.fori_loop(1, n, greet, 0)


def quarter_kernel(tok_ref, meta_ref, out_ref, info_ref, send_sem, recv_sem, own_sem):
    me, xh, yy, core = fsdp_place()
    quarter = out_ref.shape[2]
    barrier = pltpu.get_barrier_semaphore()
    for k in range(1, YS):
        pl.semaphore_signal(
            barrier,
            inc=1,
            device_id={"fsdp": fsdp_index(xh, (yy + k) % YS, core)},
            device_id_type=MESH,
        )
    pl.semaphore_wait(barrier, YS - 1)

    def part(y):
        return tok_ref.at[:, pl.ds(pl.multiple_of(y * quarter, quarter), quarter)]

    copies = []
    for k in range(1, YS):
        peer = (yy + k) % YS
        target = {"fsdp": fsdp_index(xh, peer, core)}
        for j, (source, place) in enumerate(
            ((part(peer), out_ref.at[yy]), (meta_ref, info_ref.at[yy]))
        ):
            copy = pltpu.make_async_remote_copy(
                src_ref=source,
                dst_ref=place,
                send_sem=send_sem.at[k - 1, j],
                recv_sem=recv_sem.at[k - 1, j],
                device_id=target,
                device_id_type=MESH,
            )
            copy.start()
            copies.append(copy)
    own = [
        pltpu.make_async_copy(part(yy), out_ref.at[yy], own_sem.at[0]),
        pltpu.make_async_copy(meta_ref, info_ref.at[yy], own_sem.at[1]),
    ]
    for copy in own:
        copy.start()
    for k in range(1, YS):
        origin = (yy + YS - k) % YS
        for j, place in enumerate((out_ref.at[origin], info_ref.at[origin])):
            pltpu.make_async_remote_copy(
                src_ref=place,
                dst_ref=place,
                send_sem=send_sem.at[k - 1, j],
                recv_sem=recv_sem.at[k - 1, j],
                device_id={"fsdp": fsdp_index(xh, origin, core)},
                device_id_type=MESH,
            ).wait_recv()
    for copy in copies:
        copy.wait_send()
    for copy in own:
        copy.wait()


def quarters(tok, meta, number):
    rows, width = tok.shape
    vmem = pl.BlockSpec(memory_space=pltpu.VMEM)
    return pl.pallas_call(
        quarter_kernel,
        out_shape=(
            jax.ShapeDtypeStruct((YS, rows, width // YS), tok.dtype),
            jax.ShapeDtypeStruct((YS,) + meta.shape, meta.dtype),
        ),
        in_specs=[vmem, vmem],
        out_specs=(vmem, vmem),
        scratch_shapes=[DMA((YS - 1, 2)), DMA((YS - 1, 2)), DMA((2,))],
        compiler_params=settings(number),
    )(tok, meta)


def dispatch_kernel(n, x_ref, y_ref, a_send, a_recv, send_sem, recv_sem, own_sem):
    e = lax.axis_index("expert")
    me, xh, yy, core = fsdp_place()
    tall, quarter = x_ref.shape[1], x_ref.shape[2]
    size = n // GROUPS
    other = 1 - xh
    up, down, far = (yy + 1) % YS, (yy + YS - 1) % YS, (yy + 2) % YS
    to_up, to_down = fsdp_index(xh, up, core), fsdp_index(xh, down, core)
    to_x, to_core = fsdp_index(other, yy, core), fsdp_index(xh, yy, 1 - core)

    barrier = pltpu.get_barrier_semaphore()
    for partner in (to_up, to_down, to_x, to_core):
        pl.semaphore_signal(barrier, inc=1, device_id={"fsdp": partner}, device_id_type=MESH)
    greet_all("expert", n, barrier)
    pl.semaphore_wait(barrier, n + 3)

    def place(h, y, c, first, count):
        return y_ref.at[
            h * 2 + c,
            pl.ds(pl.multiple_of(first * tall, tall), count * tall),
            pl.ds(pl.multiple_of(y * quarter, quarter), quarter),
        ]

    def hop(i, target):
        return pltpu.make_async_remote_copy(
            src_ref=x_ref.at[target],
            dst_ref=place(xh, yy, core, i, 1),
            send_sem=a_send.at[i],
            recv_sem=a_recv.at[i],
            device_id={"expert": target},
            device_id_type=MESH,
        )

    def launch(i, carry):
        hop(i, lax.rem(e + offset_of(i, n), n)).start()
        return carry

    def land(i, carry):
        hop(i, lax.rem(e + offset_of(i, n), n)).wait_recv()
        return carry

    def clear(i, carry):
        hop(i, lax.rem(e + offset_of(i, n), n)).wait_send()
        return carry

    lax.fori_loop(0, n - 1, launch, 0)
    own = pltpu.make_async_copy(x_ref.at[e], place(xh, yy, core, n - 1, 1), own_sem)
    own.start()

    sent = []

    def copy_of(h, y, c, g, target, slot):
        block = place(h, y, c, g * size, size)
        return pltpu.make_async_remote_copy(
            src_ref=block,
            dst_ref=block,
            send_sem=send_sem.at[slot],
            recv_sem=recv_sem.at[fsdp_index(h, y, c), g],
            device_id={"fsdp": target},
            device_id_type=MESH,
        )

    def send(h, y, g, *targets):
        for target in targets:
            copy = copy_of(h, y, core, g, target, len(sent))
            copy.start()
            sent.append(copy)

    def arrived(h, y, c, g):
        copy_of(h, y, c, g, to_core, 0).wait_recv()

    def from_expert(g):
        lax.fori_loop(g * size, min((g + 1) * size, n - 1), land, 0)
        if g == GROUPS - 1:
            own.wait()
        send(xh, yy, g, to_x, to_up, to_down, to_core)

    def from_x(g):
        arrived(other, yy, core, g)
        send(other, yy, g, to_up, to_down, to_core)

    def from_ring(h, g):
        for y, onward in ((down, to_up), (up, to_down)):
            arrived(h, y, core, g)
            if (g % 2 == 0) == (onward is to_up):
                send(h, y, g, onward)
            send(h, y, g, to_core)

    def from_far(h, g):
        arrived(h, far, core, g)
        send(h, far, g, to_core)

    for step in range(GROUPS + 2):
        if step < GROUPS:
            from_expert(step)
        if 1 <= step <= GROUPS:
            from_x(step - 1)
            from_ring(xh, step - 1)
        if 2 <= step:
            from_far(xh, step - 2)
            from_ring(other, step - 2)
    for g in range(GROUPS):
        from_far(other, g)
    for g in range(GROUPS):
        for h in (0, 1):
            for y in range(YS):
                arrived(h, y, 1 - core, g)
    lax.fori_loop(0, n - 1, clear, 0)
    for copy in sent:
        copy.wait_send()


def dispatch(x, n, number):
    _, tall, quarter = x.shape
    return pl.pallas_call(
        functools.partial(dispatch_kernel, n),
        out_shape=jax.ShapeDtypeStruct((4, n * tall, YS * quarter), x.dtype),
        in_specs=[ANY],
        out_specs=ANY,
        scratch_shapes=[
            DMA((n - 1,)),
            DMA((n - 1,)),
            DMA((15 * GROUPS,)),
            DMA((16, GROUPS)),
            DMA,
        ],
        compiler_params=settings(number),
    )(x)


def collect_kernel(n, m, x_ref, y_ref, rows, f_send, f_recv, a_send, a_recv, own_sem):
    e = lax.axis_index("expert")
    me = lax.axis_index("fsdp")
    width = x_ref.shape[3]
    size = n // GROUPS
    barrier = pltpu.get_barrier_semaphore()
    greet_all("fsdp", m, barrier)
    greet_all("expert", n, barrier)
    pl.semaphore_wait(barrier, n + m - 2)

    def place(first, count, block):
        return rows.at[
            pl.ds(first, count), :, pl.ds(pl.multiple_of(block * width, width), width)
        ]

    def column(i, target, origin):
        g, k = GROUPS - 1 - i // (m - 1), i % (m - 1)
        return pltpu.make_async_remote_copy(
            src_ref=x_ref.at[target, pl.ds(g * size, size)],
            dst_ref=place(g * size, size, origin),
            send_sem=f_send.at[g, k],
            recv_sem=f_recv.at[g, k],
            device_id={"fsdp": target},
            device_id_type=MESH,
        )

    def step_of(i):
        return offset_of(i % (m - 1), m)

    def column_start(i, carry):
        column(i, lax.rem(me + step_of(i), m), me).start()
        return carry

    def column_land(i, carry):
        origin = lax.rem(me - step_of(i) + m, m)
        column(i, origin, origin).wait_recv()
        return carry

    def column_clear(i, carry):
        column(i, lax.rem(me + step_of(i), m), me).wait_send()
        return carry

    own_columns = pltpu.make_async_copy(x_ref.at[me], place(0, n, me), own_sem.at[0])
    own_columns.start()
    lax.fori_loop(0, GROUPS * (m - 1), column_start, 0)
    own_columns.wait()

    def back(i, target, slot):
        return pltpu.make_async_remote_copy(
            src_ref=rows.at[i],
            dst_ref=y_ref.at[slot],
            send_sem=a_send.at[i],
            recv_sem=a_recv.at[i],
            device_id={"expert": target},
            device_id_type=MESH,
        )

    def back_start(i, carry):
        i = n - 2 - i
        back(i, lax.rem(e - offset_of(i, n) + n, n), e).start()
        return carry

    def back_finish(i, carry):
        origin = lax.rem(e + offset_of(i, n), n)
        done = back(i, origin, origin)
        done.wait_recv()
        done.wait_send()
        return carry

    for g in range(GROUPS):
        lax.fori_loop(g * (m - 1), (g + 1) * (m - 1), column_land, 0)
        lax.fori_loop(max(g * size - 1, 0), (g + 1) * size - 1, back_start, 0)
    own_rows = pltpu.make_async_copy(rows.at[n - 1], y_ref.at[e], own_sem.at[1])
    own_rows.start()
    lax.fori_loop(0, GROUPS * (m - 1), column_clear, 0)
    lax.fori_loop(0, n - 1, back_finish, 0)
    own_rows.wait()


def collect(x, n, m, number):
    _, _, slots, width = x.shape
    return pl.pallas_call(
        functools.partial(collect_kernel, n, m),
        out_shape=jax.ShapeDtypeStruct((n, slots, m * width), x.dtype),
        in_specs=[ANY],
        out_specs=ANY,
        scratch_shapes=[
            pltpu.VMEM((n, slots, m * width), x.dtype),
            DMA((GROUPS, m - 1)),
            DMA((GROUPS, m - 1)),
            DMA((n - 1,)),
            DMA((n - 1,)),
            DMA((2,)),
        ],
        compiler_params=settings(number),
    )(x)


def gather_kernel(x_ref, y_ref, send_sem, recv_sem, own_sem):
    me = lax.axis_index("fsdp")
    core, yy, xh = me % 2, (me // 2) % 4, me // 8
    half = x_ref.shape[0] // 2

    def index(h, y, c):
        return (h * 4 + y) * 2 + c

    up, down, far = (yy + 1) % 4, (yy + 3) % 4, (yy + 2) % 4
    other = 1 - xh
    to_up, to_down = index(xh, up, core), index(xh, down, core)
    to_x, to_core = index(other, yy, core), index(xh, yy, 1 - core)

    barrier = pltpu.get_barrier_semaphore()
    for partner in (to_up, to_down, to_x, to_core):
        pl.semaphore_signal(barrier, inc=1, device_id={"fsdp": partner}, device_id_type=MESH)
    pl.semaphore_wait(barrier, 4)

    sent = []

    def place(block, piece):
        return y_ref.at[block, pl.ds(piece * half, half)]

    def send(block, piece, target, own=False):
        copy = pltpu.make_async_remote_copy(
            src_ref=x_ref.at[pl.ds(piece * half, half)] if own else place(block, piece),
            dst_ref=place(block, piece),
            send_sem=send_sem.at[len(sent)],
            recv_sem=recv_sem.at[block, piece],
            device_id={"fsdp": target},
            device_id_type=MESH,
        )
        copy.start()
        sent.append(copy)

    def arrived(block, piece):
        pltpu.make_async_remote_copy(
            src_ref=place(block, piece),
            dst_ref=place(block, piece),
            send_sem=send_sem.at[0],
            recv_sem=recv_sem.at[block, piece],
            device_id={"fsdp": to_core},
            device_id_type=MESH,
        ).wait_recv()

    for piece in (0, 1):
        send(me, piece, to_x, True)
        send(me, piece, to_up, True)
        send(me, 1 - piece, to_down, True)
        send(me, piece, to_core, True)
    own = pltpu.make_async_copy(x_ref, y_ref.at[me], own_sem)
    own.start()

    def ring_first(h):
        block = index(h, down, core)
        arrived(block, 0)
        send(block, 0, to_up)
        send(block, 0, to_core)
        block = index(h, up, core)
        arrived(block, 1)
        send(block, 1, to_down)
        send(block, 1, to_core)

    def ring_rest(h):
        for block, piece in (
            (index(h, down, core), 1),
            (index(h, up, core), 0),
            (index(h, far, core), 0),
            (index(h, far, core), 1),
        ):
            arrived(block, piece)
            send(block, piece, to_core)

    ring_first(xh)
    for piece in (0, 1):
        arrived(to_x, piece)
        send(to_x, piece, to_up)
        send(to_x, piece, to_down)
        send(to_x, piece, to_core)
    ring_rest(xh)
    ring_first(other)
    ring_rest(other)
    for h in (0, 1):
        for y in range(4):
            for piece in (0, 1):
                arrived(index(h, y, 1 - core), piece)
    for copy in sent:
        copy.wait_send()
    own.wait()


def gather(x, number):
    return pl.pallas_call(
        gather_kernel,
        out_shape=jax.ShapeDtypeStruct((16,) + x.shape, x.dtype),
        in_specs=[pl.BlockSpec(memory_space=pltpu.VMEM)],
        out_specs=ANY,
        scratch_shapes=[
            pltpu.SemaphoreType.DMA((30,)),
            pltpu.SemaphoreType.DMA((16, 2)),
            pltpu.SemaphoreType.DMA,
        ],
        compiler_params=settings(number),
    )(x)


def route(expert_ids, gate_scores, experts):
    weights = gate_scores / jnp.sum(gate_scores, axis=-1, keepdims=True)
    expert_iota = lax.broadcasted_iota(jnp.int32, (1, 1, experts), 2)
    matches = (expert_ids[:, :, None] == expert_iota).astype(jnp.int32)
    chosen = jnp.sum(matches, axis=1, dtype=jnp.int32)
    weight_table = jnp.sum(weights[:, :, None] * matches.astype(jnp.float32), axis=1)
    return chosen, weight_table


def slots_of(chosen):
    ranks = jnp.cumsum(chosen, axis=-2, dtype=jnp.int32) - chosen
    slot_iota = lax.broadcasted_iota(jnp.int32, (1,) * chosen.ndim + (SLOTS,), chosen.ndim)
    return jnp.logical_and(ranks[..., None] == slot_iota, chosen[..., None] > 0)


def on_device(tokens, expert_ids, gate_scores, w_gate, w_up, w_down):
    n_expert = lax.axis_size("expert")
    n_fsdp = lax.axis_size("fsdp")
    local_tok, top_k = expert_ids.shape
    experts = n_expert
    width = tokens.shape[1]
    feature_cols = w_down.shape[2]
    tall = YS * SLOTS

    chosen, weight_table = route(expert_ids, gate_scores, experts)
    select = jnp.transpose(slots_of(chosen).astype(jnp.float32), (1, 2, 0))
    combine_table = select * jnp.transpose(weight_table)[:, None, :]

    padded = jnp.pad(tokens, ((0, 8 - local_tok), (0, 0)))
    meta = jnp.pad(chosen.astype(jnp.float32), ((0, 8 - local_tok), (0, 128 - experts)))
    tok_quarter, chosen_all = quarters(padded, meta, 0)
    masks = slots_of(chosen_all[:, :, :experts].astype(jnp.int32))
    same = jnp.eye(YS, dtype=jnp.bool_)[None, :, None, :, None]
    table = jnp.transpose(masks, (2, 0, 3, 1))[:, :, :, None, :] & same
    table = table.astype(jnp.bfloat16).reshape(experts * tall, YS * 8)
    outgoing = jnp.dot(
        table, tok_quarter.reshape(YS * 8, width // YS), preferred_element_type=jnp.float32
    )
    outgoing = outgoing.astype(jnp.bfloat16).reshape(experts, tall, width // YS)
    routed = dispatch(outgoing, n_expert, 1).reshape(4 * experts * tall, width)

    contract = (((1,), (1,)), ((), ()))
    gate_act = lax.dot_general(w_gate[0], routed, contract, preferred_element_type=jnp.float32)
    up_act = lax.dot_general(w_up[0], routed, contract, preferred_element_type=jnp.float32)
    hidden = (jax.nn.silu(gate_act) * up_act).astype(jnp.bfloat16)
    hidden = gather(hidden, 2)
    hidden = hidden.reshape(w_down.shape[1], hidden.shape[2])
    summed = lax.dot_general(
        hidden, w_down[0], (((0,), (0,)), ((), ())), preferred_element_type=jnp.float32
    )
    expert_out = summed.astype(jnp.bfloat16).reshape(2, 2, experts, YS, SLOTS, feature_cols)
    expert_out = jnp.transpose(expert_out, (0, 3, 1, 2, 4, 5))
    expert_out = expert_out.reshape(n_fsdp, experts, SLOTS, feature_cols)
    returned = collect(expert_out, n_expert, n_fsdp, 3)
    mixed = jnp.einsum(
        "ect,ecd->td", combine_table, returned.astype(jnp.float32), precision=lax.Precision.HIGHEST
    )
    return mixed.astype(jnp.bfloat16)


def solution(mesh):
    placed = (
        P(("expert", "fsdp"), None),
        P(("expert", "fsdp"), None),
        P(("expert", "fsdp"), None),
        P("expert", "fsdp", None),
        P("expert", "fsdp", None),
        P("expert", None, "fsdp"),
    )
    return jax.shard_map(
        on_device,
        mesh=mesh,
        in_specs=placed,
        out_specs=P(("expert", "fsdp"), None),
        check_vma=False,
    )
```

```python
import functools

import jax
import jax.numpy as jnp
from jax import lax
from jax.experimental import pallas as pl
from jax.experimental.pallas import tpu as pltpu
from jax.sharding import PartitionSpec as P

MESH = pl.DeviceIdType.MESH
ANY = pl.BlockSpec(memory_space=pl.ANY)
DMA = pltpu.SemaphoreType.DMA
SLOTS = 2
YS = 4
GROUPS = 4
PARTS = 8
KSTEP = 512


def fsdp_index(xh, y, core):
    return (xh * YS + y) * 2 + core


def fsdp_place():
    me = lax.axis_index("fsdp")
    return me, me // (2 * YS), (me // 2) % YS, me % 2


def settings(number):
    return pltpu.CompilerParams(
        collective_id=number, has_side_effects=True, vmem_limit_bytes=VMEM
    )


VMEM = 4 * 1024 * 1024


def offset_of(i, n):
    near = i // 2 + 1
    return near + (i % 2) * (n - 2 * near)


def greet_all(axis, n, barrier):
    me = lax.axis_index(axis)

    def greet(i, carry):
        partner = lax.rem(me + i, n)
        pl.semaphore_signal(barrier, inc=1, device_id={axis: partner}, device_id_type=MESH)
        return carry

    lax.fori_loop(1, n, greet, 0)


def quarter_kernel(tok_ref, meta_ref, out_ref, info_ref, send_sem, recv_sem, own_sem):
    me, xh, yy, core = fsdp_place()
    quarter = out_ref.shape[2]
    barrier = pltpu.get_barrier_semaphore()
    for k in range(1, YS):
        pl.semaphore_signal(
            barrier,
            inc=1,
            device_id={"fsdp": fsdp_index(xh, (yy + k) % YS, core)},
            device_id_type=MESH,
        )
    pl.semaphore_wait(barrier, YS - 1)

    def part(y):
        return tok_ref.at[:, pl.ds(pl.multiple_of(y * quarter, quarter), quarter)]

    copies = []
    for k in range(1, YS):
        peer = (yy + k) % YS
        target = {"fsdp": fsdp_index(xh, peer, core)}
        for j, (source, place) in enumerate(
            ((part(peer), out_ref.at[yy]), (meta_ref, info_ref.at[yy]))
        ):
            copy = pltpu.make_async_remote_copy(
                src_ref=source,
                dst_ref=place,
                send_sem=send_sem.at[k - 1, j],
                recv_sem=recv_sem.at[k - 1, j],
                device_id=target,
                device_id_type=MESH,
            )
            copy.start()
            copies.append(copy)
    own = [
        pltpu.make_async_copy(part(yy), out_ref.at[yy], own_sem.at[0]),
        pltpu.make_async_copy(meta_ref, info_ref.at[yy], own_sem.at[1]),
    ]
    for copy in own:
        copy.start()
    for k in range(1, YS):
        origin = (yy + YS - k) % YS
        for j, place in enumerate((out_ref.at[origin], info_ref.at[origin])):
            pltpu.make_async_remote_copy(
                src_ref=place,
                dst_ref=place,
                send_sem=send_sem.at[k - 1, j],
                recv_sem=recv_sem.at[k - 1, j],
                device_id={"fsdp": fsdp_index(xh, origin, core)},
                device_id_type=MESH,
            ).wait_recv()
    for copy in copies:
        copy.wait_send()
    for copy in own:
        copy.wait()


def quarters(tok, meta, number):
    rows, width = tok.shape
    vmem = pl.BlockSpec(memory_space=pltpu.VMEM)
    return pl.pallas_call(
        quarter_kernel,
        out_shape=(
            jax.ShapeDtypeStruct((YS, rows, width // YS), tok.dtype),
            jax.ShapeDtypeStruct((YS,) + meta.shape, meta.dtype),
        ),
        in_specs=[vmem, vmem],
        out_specs=(vmem, vmem),
        scratch_shapes=[DMA((YS - 1, 2)), DMA((YS - 1, 2)), DMA((2,))],
        compiler_params=settings(number),
    )(tok, meta)


def expert_kernel(
    n, x_ref, gate_ref, up_ref, hid_ref, routed, a_send, a_recv, t_send, t_recv, h_send, h_recv, own_sem
):
    e = lax.axis_index("expert")
    me, xh, yy, core = fsdp_place()
    tall, quarter = x_ref.shape[1], x_ref.shape[2]
    size = n // PARTS
    deep = size * tall
    cols = 4 * deep
    other = 1 - xh
    up, down, far = (yy + 1) % YS, (yy + YS - 1) % YS, (yy + 2) % YS
    to_up, to_down = fsdp_index(xh, up, core), fsdp_index(xh, down, core)
    to_x, to_core = fsdp_index(other, yy, core), fsdp_index(xh, yy, 1 - core)

    barrier = pltpu.get_barrier_semaphore()
    for partner in (to_up, to_down, to_x, to_core):
        pl.semaphore_signal(barrier, inc=1, device_id={"fsdp": partner}, device_id_type=MESH)
    greet_all("expert", n, barrier)
    pl.semaphore_wait(barrier, n + 3)

    def rows_at(h, y, c, first, count):
        return routed.at[
            h * 2 + c,
            pl.ds(pl.multiple_of(first * tall, tall), count * tall),
            pl.ds(pl.multiple_of(y * quarter, quarter), quarter),
        ]

    def hop(i):
        target = lax.rem(e + offset_of(i, n), n)
        return pltpu.make_async_remote_copy(
            src_ref=x_ref.at[target],
            dst_ref=rows_at(xh, yy, core, i, 1),
            send_sem=a_send.at[i],
            recv_sem=a_recv.at[i],
            device_id={"expert": target},
            device_id_type=MESH,
        )

    def launch(i, carry):
        hop(i).start()
        return carry

    def land(i, carry):
        hop(i).wait_recv()
        return carry

    def clear(i, carry):
        hop(i).wait_send()
        return carry

    lax.fori_loop(0, n - 1, launch, 0)
    own = pltpu.make_async_copy(x_ref.at[e], rows_at(xh, yy, core, n - 1, 1), own_sem)
    own.start()

    class Spread:
        def __init__(self, at, send_sem, recv_sem):
            self.at, self.send_sem, self.recv_sem = at, send_sem, recv_sem

        def copy(self, h, y, c, g, target, slot):
            block = self.at(h, y, c, g)
            return pltpu.make_async_remote_copy(
                src_ref=block,
                dst_ref=block,
                send_sem=self.send_sem.at[g, slot],
                recv_sem=self.recv_sem.at[fsdp_index(h, y, c), g],
                device_id={"fsdp": target},
                device_id_type=MESH,
            )

        def arrived(self, h, y, c, g):
            self.copy(h, y, c, g, to_core, 0).wait_recv()

        def first(self, g):
            for slot, target in enumerate((to_x, to_up, to_down, to_core)):
                self.copy(xh, yy, core, g, target, slot).start()

        def from_x(self, g):
            self.arrived(other, yy, core, g)
            for slot, target in enumerate((to_up, to_down, to_core)):
                self.copy(other, yy, core, g, target, 4 + slot).start()

        def from_ring(self, h, g, slot):
            self.arrived(h, down, core, g)

            @pl.when(g % 2 == 0)
            def _():
                self.copy(h, down, core, g, to_up, slot).start()

            self.copy(h, down, core, g, to_core, slot + 1).start()
            self.arrived(h, up, core, g)

            @pl.when(g % 2 == 1)
            def _():
                self.copy(h, up, core, g, to_down, slot).start()

            self.copy(h, up, core, g, to_core, slot + 2).start()

        def from_far(self, h, g, slot):
            self.arrived(h, far, core, g)
            self.copy(h, far, core, g, to_core, slot).start()

        def from_core(self, g):
            for h in (0, 1):
                for y in range(YS):
                    self.arrived(h, y, 1 - core, g)

        def drain(self, g, carry):
            for slot in range(15):
                self.copy(xh, yy, core, g, to_core, slot).wait_send()
            return carry

    tokens = Spread(lambda h, y, c, g: rows_at(h, y, c, g * size, size), t_send, t_recv)

    def columns(g):
        return pl.ds(pl.multiple_of(g * cols, cols), cols)

    hidden = Spread(lambda h, y, c, g: hid_ref.at[fsdp_index(h, y, c), :, columns(g)], h_send, h_recv)

    def compute(g):
        lines = gate_ref.shape[0]
        contract = (((1,), (1,)), ((), ()))

        def part(k, carry):
            span = pl.ds(pl.multiple_of(k * KSTEP, KSTEP), KSTEP)
            rows = routed[:, pl.ds(pl.multiple_of(g * deep, deep), deep), span]
            rows = rows.reshape(cols, KSTEP)
            return tuple(
                total
                + lax.dot_general(w[:, span], rows, contract, preferred_element_type=jnp.float32)
                for total, w in zip(carry, (gate_ref, up_ref))
            )

        zero = jnp.zeros((lines, cols), jnp.float32)
        gate, lift = lax.fori_loop(0, YS * quarter // KSTEP, part, (zero, zero))
        hid_ref[me, :, columns(g)] = (jax.nn.silu(gate) * lift).astype(hid_ref.dtype)

    def at_step(t, lag, action):
        @pl.when((t >= lag) & (t < lag + PARTS))
        def _():
            action(t - lag)

    def enter(g):
        @pl.when(g < PARTS - 1)
        def _():
            lax.fori_loop(g * size, (g + 1) * size, land, 0)

        @pl.when(g == PARTS - 1)
        def _():
            lax.fori_loop((PARTS - 1) * size, n - 1, land, 0)
            own.wait()

        tokens.first(g)

    def spread_near(group, slot):
        def action(g):
            group.from_x(g)
            group.from_ring(xh, g, slot)

        return action

    def spread_far(group, slot):
        def action(g):
            group.from_far(xh, g, slot)
            group.from_ring(other, g, slot + 1)

        return action

    def finish(g):
        tokens.from_far(other, g, 14)
        tokens.from_core(g)
        compute(g)
        hidden.first(g)

    def last(g):
        hidden.from_far(other, g, 14)

    def step(t, carry):
        at_step(t, 0, enter)
        at_step(t, 1, spread_near(tokens, 7))
        at_step(t, 2, spread_far(tokens, 10))
        at_step(t, 3, finish)
        at_step(t, 4, spread_near(hidden, 7))
        at_step(t, 5, spread_far(hidden, 10))
        at_step(t, 6, last)
        return carry

    lax.fori_loop(0, PARTS + 6, step, 0)

    def close(g, carry):
        hidden.from_core(g)
        return carry

    lax.fori_loop(0, PARTS, close, 0)
    lax.fori_loop(0, n - 1, clear, 0)
    lax.fori_loop(0, PARTS, tokens.drain, 0)
    lax.fori_loop(0, PARTS, hidden.drain, 0)


def expert_hidden(x, w_gate, w_up, n, number):
    _, tall, quarter = x.shape
    lines = w_gate.shape[0]
    vmem = pl.BlockSpec(memory_space=pltpu.VMEM)
    return pl.pallas_call(
        functools.partial(expert_kernel, n),
        out_shape=jax.ShapeDtypeStruct((16, lines, 4 * n * tall), x.dtype),
        in_specs=[ANY, vmem, vmem],
        out_specs=vmem,
        scratch_shapes=[
            pltpu.VMEM((4, n * tall, YS * quarter), x.dtype),
            DMA((n - 1,)),
            DMA((n - 1,)),
            DMA((PARTS, 15)),
            DMA((16, PARTS)),
            DMA((PARTS, 15)),
            DMA((16, PARTS)),
            DMA,
        ],
        compiler_params=pltpu.CompilerParams(
            collective_id=number, has_side_effects=True, vmem_limit_bytes=6 * VMEM
        ),
    )(x, w_gate, w_up)


def collect_kernel(n, m, x_ref, y_ref, rows, f_send, f_recv, a_send, a_recv, own_sem):
    e = lax.axis_index("expert")
    me = lax.axis_index("fsdp")
    width = x_ref.shape[3]
    size = n // GROUPS
    barrier = pltpu.get_barrier_semaphore()
    greet_all("fsdp", m, barrier)
    greet_all("expert", n, barrier)
    pl.semaphore_wait(barrier, n + m - 2)

    def place(first, count, block):
        return rows.at[
            pl.ds(first, count), :, pl.ds(pl.multiple_of(block * width, width), width)
        ]

    def column(i, target, origin):
        g, k = GROUPS - 1 - i // (m - 1), i % (m - 1)
        return pltpu.make_async_remote_copy(
            src_ref=x_ref.at[target, pl.ds(g * size, size)],
            dst_ref=place(g * size, size, origin),
            send_sem=f_send.at[g, k],
            recv_sem=f_recv.at[g, k],
            device_id={"fsdp": target},
            device_id_type=MESH,
        )

    def step_of(i):
        return offset_of(i % (m - 1), m)

    def column_start(i, carry):
        column(i, lax.rem(me + step_of(i), m), me).start()
        return carry

    def column_land(i, carry):
        origin = lax.rem(me - step_of(i) + m, m)
        column(i, origin, origin).wait_recv()
        return carry

    def column_clear(i, carry):
        column(i, lax.rem(me + step_of(i), m), me).wait_send()
        return carry

    own_columns = pltpu.make_async_copy(x_ref.at[me], place(0, n, me), own_sem.at[0])
    own_columns.start()
    lax.fori_loop(0, GROUPS * (m - 1), column_start, 0)
    own_columns.wait()

    def back(i, target, slot):
        return pltpu.make_async_remote_copy(
            src_ref=rows.at[i],
            dst_ref=y_ref.at[slot],
            send_sem=a_send.at[i],
            recv_sem=a_recv.at[i],
            device_id={"expert": target},
            device_id_type=MESH,
        )

    def back_start(i, carry):
        i = n - 2 - i
        back(i, lax.rem(e - offset_of(i, n) + n, n), e).start()
        return carry

    def back_finish(i, carry):
        origin = lax.rem(e + offset_of(i, n), n)
        done = back(i, origin, origin)
        done.wait_recv()
        done.wait_send()
        return carry

    for g in range(GROUPS):
        lax.fori_loop(g * (m - 1), (g + 1) * (m - 1), column_land, 0)
        lax.fori_loop(max(g * size - 1, 0), (g + 1) * size - 1, back_start, 0)
    own_rows = pltpu.make_async_copy(rows.at[n - 1], y_ref.at[e], own_sem.at[1])
    own_rows.start()
    lax.fori_loop(0, GROUPS * (m - 1), column_clear, 0)
    lax.fori_loop(0, n - 1, back_finish, 0)
    own_rows.wait()


def collect(x, n, m, number):
    _, _, slots, width = x.shape
    return pl.pallas_call(
        functools.partial(collect_kernel, n, m),
        out_shape=jax.ShapeDtypeStruct((n, slots, m * width), x.dtype),
        in_specs=[ANY],
        out_specs=ANY,
        scratch_shapes=[
            pltpu.VMEM((n, slots, m * width), x.dtype),
            DMA((GROUPS, m - 1)),
            DMA((GROUPS, m - 1)),
            DMA((n - 1,)),
            DMA((n - 1,)),
            DMA((2,)),
        ],
        compiler_params=settings(number),
    )(x)


def route(expert_ids, gate_scores, experts):
    weights = gate_scores / jnp.sum(gate_scores, axis=-1, keepdims=True)
    expert_iota = lax.broadcasted_iota(jnp.int32, (1, 1, experts), 2)
    matches = (expert_ids[:, :, None] == expert_iota).astype(jnp.int32)
    chosen = jnp.sum(matches, axis=1, dtype=jnp.int32)
    weight_table = jnp.sum(weights[:, :, None] * matches.astype(jnp.float32), axis=1)
    return chosen, weight_table


def slots_of(chosen):
    ranks = jnp.cumsum(chosen, axis=-2, dtype=jnp.int32) - chosen
    slot_iota = lax.broadcasted_iota(jnp.int32, (1,) * chosen.ndim + (SLOTS,), chosen.ndim)
    return jnp.logical_and(ranks[..., None] == slot_iota, chosen[..., None] > 0)


def on_device(tokens, expert_ids, gate_scores, w_gate, w_up, w_down):
    n_expert = lax.axis_size("expert")
    n_fsdp = lax.axis_size("fsdp")
    local_tok, top_k = expert_ids.shape
    experts = n_expert
    width = tokens.shape[1]
    feature_cols = w_down.shape[2]
    tall = YS * SLOTS

    chosen, weight_table = route(expert_ids, gate_scores, experts)
    select = jnp.transpose(slots_of(chosen).astype(jnp.float32), (1, 2, 0))
    combine_table = select * jnp.transpose(weight_table)[:, None, :]

    padded = jnp.pad(tokens, ((0, 8 - local_tok), (0, 0)))
    meta = jnp.pad(chosen.astype(jnp.float32), ((0, 8 - local_tok), (0, 128 - experts)))
    tok_quarter, chosen_all = quarters(padded, meta, 0)
    masks = slots_of(chosen_all[:, :, :experts].astype(jnp.int32))
    same = jnp.eye(YS, dtype=jnp.bool_)[None, :, None, :, None]
    table = jnp.transpose(masks, (2, 0, 3, 1))[:, :, :, None, :] & same
    table = table.astype(jnp.bfloat16).reshape(experts * tall, YS * 8)
    outgoing = jnp.dot(
        table, tok_quarter.reshape(YS * 8, width // YS), preferred_element_type=jnp.float32
    )
    outgoing = outgoing.astype(jnp.bfloat16).reshape(experts, tall, width // YS)
    hidden = expert_hidden(outgoing, w_gate[0], w_up[0], n_expert, 1)
    hidden = hidden.reshape(w_down.shape[1], hidden.shape[2])
    summed = lax.dot_general(
        hidden, w_down[0], (((0,), (0,)), ((), ())), preferred_element_type=jnp.float32
    )
    expert_out = summed.astype(jnp.bfloat16)
    expert_out = expert_out.reshape(PARTS, 2, 2, experts // PARTS, YS, SLOTS, feature_cols)
    expert_out = jnp.transpose(expert_out, (1, 4, 2, 0, 3, 5, 6))
    expert_out = expert_out.reshape(n_fsdp, experts, SLOTS, feature_cols)
    returned = collect(expert_out, n_expert, n_fsdp, 3)
    mixed = jnp.einsum(
        "ect,ecd->td", combine_table, returned.astype(jnp.float32), precision=lax.Precision.HIGHEST
    )
    return mixed.astype(jnp.bfloat16)


def solution(mesh):
    placed = (
        P(("expert", "fsdp"), None),
        P(("expert", "fsdp"), None),
        P(("expert", "fsdp"), None),
        P("expert", "fsdp", None),
        P("expert", "fsdp", None),
        P("expert", None, "fsdp"),
    )
    return jax.shard_map(
        on_device,
        mesh=mesh,
        in_specs=placed,
        out_specs=P(("expert", "fsdp"), None),
        check_vma=False,
    )
```

```python
import functools

import jax
import jax.numpy as jnp
from jax import lax
from jax.experimental import pallas as pl
from jax.experimental.pallas import tpu as pltpu
from jax.sharding import PartitionSpec as P

MESH = pl.DeviceIdType.MESH
ANY = pl.BlockSpec(memory_space=pl.ANY)
DMA = pltpu.SemaphoreType.DMA
SLOTS = 2
YS = 4
PARTS = 8
KSTEP = 512


def fsdp_index(xh, y, core):
    return (xh * YS + y) * 2 + core


def fsdp_place():
    me = lax.axis_index("fsdp")
    return me, me // (2 * YS), (me // 2) % YS, me % 2


def settings(number):
    return pltpu.CompilerParams(
        collective_id=number, has_side_effects=True, vmem_limit_bytes=VMEM
    )


VMEM = 4 * 1024 * 1024


def offset_of(i, n):
    near = i // 2 + 1
    return near + (i % 2) * (n - 2 * near)


def greet_all(axis, n, barrier):
    me = lax.axis_index(axis)

    def greet(i, carry):
        partner = lax.rem(me + i, n)
        pl.semaphore_signal(barrier, inc=1, device_id={axis: partner}, device_id_type=MESH)
        return carry

    lax.fori_loop(1, n, greet, 0)


def quarter_kernel(tok_ref, meta_ref, out_ref, info_ref, send_sem, recv_sem, own_sem):
    me, xh, yy, core = fsdp_place()
    quarter = out_ref.shape[2]
    barrier = pltpu.get_barrier_semaphore()
    for k in range(1, YS):
        pl.semaphore_signal(
            barrier,
            inc=1,
            device_id={"fsdp": fsdp_index(xh, (yy + k) % YS, core)},
            device_id_type=MESH,
        )
    pl.semaphore_wait(barrier, YS - 1)

    def part(y):
        return tok_ref.at[:, pl.ds(pl.multiple_of(y * quarter, quarter), quarter)]

    copies = []
    for k in range(1, YS):
        peer = (yy + k) % YS
        target = {"fsdp": fsdp_index(xh, peer, core)}
        for j, (source, place) in enumerate(
            ((part(peer), out_ref.at[yy]), (meta_ref, info_ref.at[yy]))
        ):
            copy = pltpu.make_async_remote_copy(
                src_ref=source,
                dst_ref=place,
                send_sem=send_sem.at[k - 1, j],
                recv_sem=recv_sem.at[k - 1, j],
                device_id=target,
                device_id_type=MESH,
            )
            copy.start()
            copies.append(copy)
    own = [
        pltpu.make_async_copy(part(yy), out_ref.at[yy], own_sem.at[0]),
        pltpu.make_async_copy(meta_ref, info_ref.at[yy], own_sem.at[1]),
    ]
    for copy in own:
        copy.start()
    for k in range(1, YS):
        origin = (yy + YS - k) % YS
        for j, place in enumerate((out_ref.at[origin], info_ref.at[origin])):
            pltpu.make_async_remote_copy(
                src_ref=place,
                dst_ref=place,
                send_sem=send_sem.at[k - 1, j],
                recv_sem=recv_sem.at[k - 1, j],
                device_id={"fsdp": fsdp_index(xh, origin, core)},
                device_id_type=MESH,
            ).wait_recv()
    for copy in copies:
        copy.wait_send()
    for copy in own:
        copy.wait()


def quarters(tok, meta, number):
    rows, width = tok.shape
    vmem = pl.BlockSpec(memory_space=pltpu.VMEM)
    return pl.pallas_call(
        quarter_kernel,
        out_shape=(
            jax.ShapeDtypeStruct((YS, rows, width // YS), tok.dtype),
            jax.ShapeDtypeStruct((YS,) + meta.shape, meta.dtype),
        ),
        in_specs=[vmem, vmem],
        out_specs=(vmem, vmem),
        scratch_shapes=[DMA((YS - 1, 2)), DMA((YS - 1, 2)), DMA((2,))],
        compiler_params=settings(number),
    )(tok, meta)


def expert_kernel(
    n,
    m,
    x_ref,
    gate_ref,
    up_ref,
    down_ref,
    y_ref,
    routed,
    hid_ref,
    stage,
    rows,
    a_send,
    a_recv,
    t_send,
    t_recv,
    h_send,
    h_recv,
    c_send,
    c_recv,
    b_send,
    b_recv,
    own_sem,
    mine_sem,
):
    e = lax.axis_index("expert")
    me, xh, yy, core = fsdp_place()
    tall, quarter = x_ref.shape[1], x_ref.shape[2]
    size = n // PARTS
    deep = size * tall
    cols = 4 * deep
    other = 1 - xh
    up, down, far = (yy + 1) % YS, (yy + YS - 1) % YS, (yy + 2) % YS
    to_up, to_down = fsdp_index(xh, up, core), fsdp_index(xh, down, core)
    to_x, to_core = fsdp_index(other, yy, core), fsdp_index(xh, yy, 1 - core)

    barrier = pltpu.get_barrier_semaphore()
    greet_all("fsdp", m, barrier)
    greet_all("expert", n, barrier)
    pl.semaphore_wait(barrier, n + m - 2)

    def rows_at(h, y, c, first, count):
        return routed.at[
            h * 2 + c,
            pl.ds(pl.multiple_of(first * tall, tall), count * tall),
            pl.ds(pl.multiple_of(y * quarter, quarter), quarter),
        ]

    def hop(i):
        target = lax.rem(e + offset_of(i, n), n)
        return pltpu.make_async_remote_copy(
            src_ref=x_ref.at[target],
            dst_ref=rows_at(xh, yy, core, i, 1),
            send_sem=a_send.at[i],
            recv_sem=a_recv.at[i],
            device_id={"expert": target},
            device_id_type=MESH,
        )

    def launch(i, carry):
        hop(i).start()
        return carry

    def land(i, carry):
        hop(i).wait_recv()
        return carry

    def clear(i, carry):
        hop(i).wait_send()
        return carry

    lax.fori_loop(0, n - 1, launch, 0)
    own = pltpu.make_async_copy(x_ref.at[e], rows_at(xh, yy, core, n - 1, 1), own_sem.at[0])
    own.start()

    class Spread:
        def __init__(self, at, send_sem, recv_sem):
            self.at, self.send_sem, self.recv_sem = at, send_sem, recv_sem

        def copy(self, h, y, c, g, target, slot):
            block = self.at(h, y, c, g)
            return pltpu.make_async_remote_copy(
                src_ref=block,
                dst_ref=block,
                send_sem=self.send_sem.at[g, slot],
                recv_sem=self.recv_sem.at[fsdp_index(h, y, c), g],
                device_id={"fsdp": target},
                device_id_type=MESH,
            )

        def arrived(self, h, y, c, g):
            self.copy(h, y, c, g, to_core, 0).wait_recv()

        def first(self, g):
            for slot, target in enumerate((to_x, to_up, to_down, to_core)):
                self.copy(xh, yy, core, g, target, slot).start()

        def from_x(self, g):
            self.arrived(other, yy, core, g)
            for slot, target in enumerate((to_up, to_down, to_core)):
                self.copy(other, yy, core, g, target, 4 + slot).start()

        def from_ring(self, h, g, slot):
            self.arrived(h, down, core, g)

            @pl.when(g % 2 == 0)
            def _():
                self.copy(h, down, core, g, to_up, slot).start()

            self.copy(h, down, core, g, to_core, slot + 1).start()
            self.arrived(h, up, core, g)

            @pl.when(g % 2 == 1)
            def _():
                self.copy(h, up, core, g, to_down, slot).start()

            self.copy(h, up, core, g, to_core, slot + 2).start()

        def from_far(self, h, g, slot):
            self.arrived(h, far, core, g)
            self.copy(h, far, core, g, to_core, slot).start()

        def from_core(self, g):
            for h in (0, 1):
                for y in range(YS):
                    self.arrived(h, y, 1 - core, g)

        def drain(self, g, carry):
            for slot in range(15):
                self.copy(xh, yy, core, g, to_core, slot).wait_send()
            return carry

    tokens = Spread(lambda h, y, c, g: rows_at(h, y, c, g * size, size), t_send, t_recv)

    def columns(g):
        return pl.ds(pl.multiple_of(g * cols, cols), cols)

    hidden = Spread(lambda h, y, c, g: hid_ref.at[fsdp_index(h, y, c), :, columns(g)], h_send, h_recv)

    def compute(g):
        lines = gate_ref.shape[0]
        contract = (((1,), (1,)), ((), ()))

        def part(k, carry):
            span = pl.ds(pl.multiple_of(k * KSTEP, KSTEP), KSTEP)
            rows = routed[:, pl.ds(pl.multiple_of(g * deep, deep), deep), span]
            rows = rows.reshape(cols, KSTEP)
            return tuple(
                total
                + lax.dot_general(w[:, span], rows, contract, preferred_element_type=jnp.float32)
                for total, w in zip(carry, (gate_ref, up_ref))
            )

        zero = jnp.zeros((lines, cols), jnp.float32)
        gate, lift = lax.fori_loop(0, YS * quarter // KSTEP, part, (zero, zero))
        hid_ref[me, :, columns(g)] = (jax.nn.silu(gate) * lift).astype(hid_ref.dtype)

    def at_step(t, lag, action):
        @pl.when((t >= lag) & (t < lag + PARTS))
        def _():
            action(t - lag)

    def enter(g):
        @pl.when(g < PARTS - 1)
        def _():
            lax.fori_loop(g * size, (g + 1) * size, land, 0)

        @pl.when(g == PARTS - 1)
        def _():
            lax.fori_loop((PARTS - 1) * size, n - 1, land, 0)
            own.wait()

        tokens.first(g)

    def spread_near(group, slot):
        def action(g):
            group.from_x(g)
            group.from_ring(xh, g, slot)

        return action

    def spread_far(group, slot):
        def action(g):
            group.from_far(xh, g, slot)
            group.from_ring(other, g, slot + 1)

        return action

    def finish(g):
        tokens.from_far(other, g, 14)
        tokens.from_core(g)
        compute(g)
        hidden.first(g)

    width = down_ref.shape[1]
    lines = gate_ref.shape[0]

    def compute_out(g):
        deepk = 4 * lines

        def part(k, total):
            left = hid_ref[pl.ds(k * 4, 4), :, columns(g)].reshape(deepk, cols)
            right = down_ref[pl.ds(pl.multiple_of(k * deepk, deepk), deepk), :]
            return total + lax.dot_general(
                left, right, (((0,), (0,)), ((), ())), preferred_element_type=jnp.float32
            )

        out = lax.fori_loop(0, m // 4, part, jnp.zeros((cols, width), jnp.float32))
        for b in range(4):
            for i in range(size):
                for y in range(YS):
                    row = (b * size + i) * tall + y * SLOTS
                    target = fsdp_index(b // 2, y, b % 2)
                    stage[target, g * size + i] = out[row : row + SLOTS].astype(stage.dtype)

    def column_place(g, block):
        return rows.at[
            pl.ds(g * size, size), :, pl.ds(pl.multiple_of(block * width, width), width)
        ]

    def column(g, k, target, origin):
        return pltpu.make_async_remote_copy(
            src_ref=stage.at[target, pl.ds(g * size, size)],
            dst_ref=column_place(g, origin),
            send_sem=c_send.at[g, k],
            recv_sem=c_recv.at[g, k],
            device_id={"fsdp": target},
            device_id_type=MESH,
        )

    def mine(g):
        return pltpu.make_async_copy(
            stage.at[me, pl.ds(g * size, size)], column_place(g, me), mine_sem.at[g]
        )

    def last(g):
        hidden.from_far(other, g, 14)
        hidden.from_core(g)
        compute_out(g)

        def column_start(k, carry):
            column(g, k, lax.rem(me + 1 + k, m), me).start()
            return carry

        lax.fori_loop(0, m - 1, column_start, 0)
        mine(g).start()

    def back(i, target, slot):
        return pltpu.make_async_remote_copy(
            src_ref=rows.at[i],
            dst_ref=y_ref.at[slot],
            send_sem=b_send.at[i],
            recv_sem=b_recv.at[i],
            device_id={"expert": target},
            device_id_type=MESH,
        )

    own_rows = pltpu.make_async_copy(rows.at[n - 1], y_ref.at[e], own_sem.at[1])

    def give_back(g):
        def column_land(k, carry):
            origin = lax.rem(me - 1 - k + m, m)
            column(g, k, origin, origin).wait_recv()
            return carry

        def back_start(i, carry):
            back(i, lax.rem(e - offset_of(i, n) + n, n), e).start()
            return carry

        lax.fori_loop(0, m - 1, column_land, 0)
        mine(g).wait()

        @pl.when(g < PARTS - 1)
        def _():
            lax.fori_loop(g * size, (g + 1) * size, back_start, 0)

        @pl.when(g == PARTS - 1)
        def _():
            lax.fori_loop((PARTS - 1) * size, n - 1, back_start, 0)
            own_rows.start()

    def step(t, carry):
        at_step(t, 0, enter)
        at_step(t, 1, spread_near(tokens, 7))
        at_step(t, 2, spread_far(tokens, 10))
        at_step(t, 3, finish)
        at_step(t, 4, spread_near(hidden, 7))
        at_step(t, 5, spread_far(hidden, 10))
        at_step(t, 6, last)
        at_step(t, 7, give_back)
        return carry

    lax.fori_loop(0, PARTS + 7, step, 0)

    def column_clear(g, carry):
        def one(k, inner):
            column(g, k, lax.rem(me + 1 + k, m), me).wait_send()
            return inner

        return lax.fori_loop(0, m - 1, one, carry)

    def back_finish(i, carry):
        origin = lax.rem(e + offset_of(i, n), n)
        done = back(i, origin, origin)
        done.wait_recv()
        done.wait_send()
        return carry

    lax.fori_loop(0, n - 1, clear, 0)
    lax.fori_loop(0, PARTS, tokens.drain, 0)
    lax.fori_loop(0, PARTS, hidden.drain, 0)
    lax.fori_loop(0, PARTS, column_clear, 0)
    lax.fori_loop(0, n - 1, back_finish, 0)
    own_rows.wait()


def experts_round(x, w_gate, w_up, w_down, n, m, number):
    _, tall, quarter = x.shape
    lines = w_gate.shape[0]
    width = YS * quarter
    vmem = pl.BlockSpec(memory_space=pltpu.VMEM)
    return pl.pallas_call(
        functools.partial(expert_kernel, n, m),
        out_shape=jax.ShapeDtypeStruct((n, SLOTS, width), x.dtype),
        in_specs=[ANY, vmem, vmem, vmem],
        out_specs=ANY,
        scratch_shapes=[
            pltpu.VMEM((4, n * tall, width), x.dtype),
            pltpu.VMEM((m, lines, 4 * n * tall), x.dtype),
            pltpu.VMEM((m, n, SLOTS, width // m), x.dtype),
            pltpu.VMEM((n, SLOTS, width), x.dtype),
            DMA((n - 1,)),
            DMA((n - 1,)),
            DMA((PARTS, 15)),
            DMA((m, PARTS)),
            DMA((PARTS, 15)),
            DMA((m, PARTS)),
            DMA((PARTS, m - 1)),
            DMA((PARTS, m - 1)),
            DMA((n - 1,)),
            DMA((n - 1,)),
            DMA((2,)),
            DMA((PARTS,)),
        ],
        compiler_params=pltpu.CompilerParams(
            collective_id=number, has_side_effects=True, vmem_limit_bytes=8 * VMEM
        ),
    )(x, w_gate, w_up, w_down)


def route(expert_ids, gate_scores, experts):
    weights = gate_scores / jnp.sum(gate_scores, axis=-1, keepdims=True)
    expert_iota = lax.broadcasted_iota(jnp.int32, (1, 1, experts), 2)
    matches = (expert_ids[:, :, None] == expert_iota).astype(jnp.int32)
    chosen = jnp.sum(matches, axis=1, dtype=jnp.int32)
    weight_table = jnp.sum(weights[:, :, None] * matches.astype(jnp.float32), axis=1)
    return chosen, weight_table


def slots_of(chosen):
    ranks = jnp.cumsum(chosen, axis=-2, dtype=jnp.int32) - chosen
    slot_iota = lax.broadcasted_iota(jnp.int32, (1,) * chosen.ndim + (SLOTS,), chosen.ndim)
    return jnp.logical_and(ranks[..., None] == slot_iota, chosen[..., None] > 0)


def on_device(tokens, expert_ids, gate_scores, w_gate, w_up, w_down):
    n_expert = lax.axis_size("expert")
    n_fsdp = lax.axis_size("fsdp")
    local_tok, top_k = expert_ids.shape
    experts = n_expert
    width = tokens.shape[1]
    tall = YS * SLOTS

    chosen, weight_table = route(expert_ids, gate_scores, experts)
    select = jnp.transpose(slots_of(chosen).astype(jnp.float32), (1, 2, 0))
    combine_table = select * jnp.transpose(weight_table)[:, None, :]

    padded = jnp.pad(tokens, ((0, 8 - local_tok), (0, 0)))
    meta = jnp.pad(chosen.astype(jnp.float32), ((0, 8 - local_tok), (0, 128 - experts)))
    tok_quarter, chosen_all = quarters(padded, meta, 0)
    masks = slots_of(chosen_all[:, :, :experts].astype(jnp.int32))
    same = jnp.eye(YS, dtype=jnp.bool_)[None, :, None, :, None]
    table = jnp.transpose(masks, (2, 0, 3, 1))[:, :, :, None, :] & same
    table = table.astype(jnp.bfloat16).reshape(experts * tall, YS * 8)
    outgoing = jnp.dot(
        table, tok_quarter.reshape(YS * 8, width // YS), preferred_element_type=jnp.float32
    )
    outgoing = outgoing.astype(jnp.bfloat16).reshape(experts, tall, width // YS)
    returned = experts_round(
        outgoing, w_gate[0], w_up[0], w_down[0], n_expert, n_fsdp, 1
    )
    mixed = jnp.einsum(
        "ect,ecd->td", combine_table, returned.astype(jnp.float32), precision=lax.Precision.HIGHEST
    )
    return mixed.astype(jnp.bfloat16)


def solution(mesh):
    placed = (
        P(("expert", "fsdp"), None),
        P(("expert", "fsdp"), None),
        P(("expert", "fsdp"), None),
        P("expert", "fsdp", None),
        P("expert", "fsdp", None),
        P("expert", None, "fsdp"),
    )
    return jax.shard_map(
        on_device,
        mesh=mesh,
        in_specs=placed,
        out_specs=P(("expert", "fsdp"), None),
        check_vma=False,
    )
```

```python
import functools

import jax
import jax.numpy as jnp
from jax import lax
from jax.experimental import pallas as pl
from jax.experimental.pallas import tpu as pltpu
from jax.sharding import PartitionSpec as P

MESH = pl.DeviceIdType.MESH
ANY = pl.BlockSpec(memory_space=pl.ANY)
DMA = pltpu.SemaphoreType.DMA
SLOTS = 2
YS = 4
PARTS = 8
KSTEP = 1024


def fsdp_index(xh, y, core):
    return (xh * YS + y) * 2 + core


def fsdp_place():
    me = lax.axis_index("fsdp")
    return me, me // (2 * YS), (me // 2) % YS, me % 2


def settings(number):
    return pltpu.CompilerParams(
        collective_id=number, has_side_effects=True, vmem_limit_bytes=VMEM
    )


VMEM = 4 * 1024 * 1024


def offset_of(i, n):
    head = n // 4
    beyond = (i + n - head) // n
    place = i + beyond * (n + head - 2 - 2 * i)
    near = place // 2 + 1
    return near + (place % 2) * (n - 2 * near)


def greet_all(axis, n, barrier):
    me = lax.axis_index(axis)

    def greet(i, carry):
        partner = lax.rem(me + i, n)
        pl.semaphore_signal(barrier, inc=1, device_id={axis: partner}, device_id_type=MESH)
        return carry

    lax.fori_loop(1, n, greet, 0)


def quarter_kernel(tok_ref, meta_ref, out_ref, info_ref, send_sem, recv_sem, own_sem):
    me, xh, yy, core = fsdp_place()
    quarter = out_ref.shape[2]
    barrier = pltpu.get_barrier_semaphore()
    for k in range(1, YS):
        pl.semaphore_signal(
            barrier,
            inc=1,
            device_id={"fsdp": fsdp_index(xh, (yy + k) % YS, core)},
            device_id_type=MESH,
        )
    pl.semaphore_wait(barrier, YS - 1)

    def part(y):
        return tok_ref.at[:, pl.ds(pl.multiple_of(y * quarter, quarter), quarter)]

    copies = []
    for k in range(1, YS):
        peer = (yy + k) % YS
        target = {"fsdp": fsdp_index(xh, peer, core)}
        for j, (source, place) in enumerate(
            ((part(peer), out_ref.at[yy]), (meta_ref, info_ref.at[yy]))
        ):
            copy = pltpu.make_async_remote_copy(
                src_ref=source,
                dst_ref=place,
                send_sem=send_sem.at[k - 1, j],
                recv_sem=recv_sem.at[k - 1, j],
                device_id=target,
                device_id_type=MESH,
            )
            copy.start()
            copies.append(copy)
    own = [
        pltpu.make_async_copy(part(yy), out_ref.at[yy], own_sem.at[0]),
        pltpu.make_async_copy(meta_ref, info_ref.at[yy], own_sem.at[1]),
    ]
    for copy in own:
        copy.start()
    for k in range(1, YS):
        origin = (yy + YS - k) % YS
        for j, place in enumerate((out_ref.at[origin], info_ref.at[origin])):
            pltpu.make_async_remote_copy(
                src_ref=place,
                dst_ref=place,
                send_sem=send_sem.at[k - 1, j],
                recv_sem=recv_sem.at[k - 1, j],
                device_id={"fsdp": fsdp_index(xh, origin, core)},
                device_id_type=MESH,
            ).wait_recv()
    for copy in copies:
        copy.wait_send()
    for copy in own:
        copy.wait()


def quarters(tok, meta, number):
    rows, width = tok.shape
    vmem = pl.BlockSpec(memory_space=pltpu.VMEM)
    return pl.pallas_call(
        quarter_kernel,
        out_shape=(
            jax.ShapeDtypeStruct((YS, rows, width // YS), tok.dtype),
            jax.ShapeDtypeStruct((YS,) + meta.shape, meta.dtype),
        ),
        in_specs=[vmem, vmem],
        out_specs=(vmem, vmem),
        scratch_shapes=[DMA((YS - 1, 2)), DMA((YS - 1, 2)), DMA((2,))],
        compiler_params=settings(number),
    )(tok, meta)


def expert_kernel(
    n,
    m,
    x_ref,
    gate_ref,
    up_ref,
    down_ref,
    y_ref,
    routed,
    hid_ref,
    stage,
    rows,
    a_send,
    a_recv,
    t_send,
    t_recv,
    h_send,
    h_recv,
    c_send,
    c_recv,
    b_send,
    b_recv,
    own_sem,
    mine_sem,
):
    e = lax.axis_index("expert")
    me, xh, yy, core = fsdp_place()
    tall, quarter = x_ref.shape[1], x_ref.shape[2]
    size = n // PARTS
    deep = size * tall
    cols = 4 * deep
    other = 1 - xh
    up, down, far = (yy + 1) % YS, (yy + YS - 1) % YS, (yy + 2) % YS
    to_up, to_down = fsdp_index(xh, up, core), fsdp_index(xh, down, core)
    to_x, to_core = fsdp_index(other, yy, core), fsdp_index(xh, yy, 1 - core)

    barrier = pltpu.get_barrier_semaphore()
    greet_all("fsdp", m, barrier)
    greet_all("expert", n, barrier)
    pl.semaphore_wait(barrier, n + m - 2)

    def rows_at(h, y, c, first, count):
        return routed.at[
            h * 2 + c,
            pl.ds(pl.multiple_of(first * tall, tall), count * tall),
            pl.ds(pl.multiple_of(y * quarter, quarter), quarter),
        ]

    def hop(i):
        target = lax.rem(e + offset_of(i, n), n)
        return pltpu.make_async_remote_copy(
            src_ref=x_ref.at[target],
            dst_ref=rows_at(xh, yy, core, i, 1),
            send_sem=a_send.at[i],
            recv_sem=a_recv.at[i],
            device_id={"expert": target},
            device_id_type=MESH,
        )

    def launch(i, carry):
        hop(i).start()
        return carry

    def land(i, carry):
        hop(i).wait_recv()
        return carry

    def clear(i, carry):
        hop(i).wait_send()
        return carry

    lax.fori_loop(0, n - 1, launch, 0)
    own = pltpu.make_async_copy(x_ref.at[e], rows_at(xh, yy, core, n - 1, 1), own_sem.at[0])
    own.start()

    class Spread:
        def __init__(self, at, send_sem, recv_sem):
            self.at, self.send_sem, self.recv_sem = at, send_sem, recv_sem

        def copy(self, h, y, c, g, target, slot):
            block = self.at(h, y, c, g)
            return pltpu.make_async_remote_copy(
                src_ref=block,
                dst_ref=block,
                send_sem=self.send_sem.at[g, slot],
                recv_sem=self.recv_sem.at[fsdp_index(h, y, c), g],
                device_id={"fsdp": target},
                device_id_type=MESH,
            )

        def arrived(self, h, y, c, g):
            self.copy(h, y, c, g, to_core, 0).wait_recv()

        def first(self, g):
            for slot, target in enumerate((to_x, to_up, to_down, to_core)):
                self.copy(xh, yy, core, g, target, slot).start()

        def from_x(self, g):
            self.arrived(other, yy, core, g)
            for slot, target in enumerate((to_up, to_down, to_core)):
                self.copy(other, yy, core, g, target, 4 + slot).start()

        def from_ring(self, h, g, slot):
            self.arrived(h, down, core, g)

            @pl.when(g % 2 == 0)
            def _():
                self.copy(h, down, core, g, to_up, slot).start()

            self.copy(h, down, core, g, to_core, slot + 1).start()
            self.arrived(h, up, core, g)

            @pl.when(g % 2 == 1)
            def _():
                self.copy(h, up, core, g, to_down, slot).start()

            self.copy(h, up, core, g, to_core, slot + 2).start()

        def from_far(self, h, g, slot):
            self.arrived(h, far, core, g)
            self.copy(h, far, core, g, to_core, slot).start()

        def from_core(self, g):
            for h in (0, 1):
                for y in range(YS):
                    self.arrived(h, y, 1 - core, g)

        def drain(self, g, carry):
            for slot in range(15):
                self.copy(xh, yy, core, g, to_core, slot).wait_send()
            return carry

    tokens = Spread(lambda h, y, c, g: rows_at(h, y, c, g * size, size), t_send, t_recv)

    def columns(g):
        return pl.ds(pl.multiple_of(g * cols, cols), cols)

    hidden = Spread(lambda h, y, c, g: hid_ref.at[fsdp_index(h, y, c), :, columns(g)], h_send, h_recv)

    def compute(g):
        lines = gate_ref.shape[0]
        contract = (((1,), (1,)), ((), ()))

        def part(k, carry):
            span = pl.ds(pl.multiple_of(k * KSTEP, KSTEP), KSTEP)
            rows = routed[:, pl.ds(pl.multiple_of(g * deep, deep), deep), span]
            rows = rows.reshape(cols, KSTEP)
            return tuple(
                total
                + lax.dot_general(w[:, span], rows, contract, preferred_element_type=jnp.float32)
                for total, w in zip(carry, (gate_ref, up_ref))
            )

        zero = jnp.zeros((lines, cols), jnp.float32)
        gate, lift = lax.fori_loop(0, YS * quarter // KSTEP, part, (zero, zero))
        hid_ref[me, :, columns(g)] = (jax.nn.silu(gate) * lift).astype(hid_ref.dtype)

    def at_step(t, lag, action):
        @pl.when((t >= lag) & (t < lag + PARTS))
        def _():
            action(t - lag)

    def enter(g):
        @pl.when(g < PARTS - 1)
        def _():
            lax.fori_loop(g * size, (g + 1) * size, land, 0)

        @pl.when(g == PARTS - 1)
        def _():
            lax.fori_loop((PARTS - 1) * size, n - 1, land, 0)
            own.wait()

        tokens.first(g)

    def spread_near(group, slot):
        def action(g):
            group.from_x(g)
            group.from_ring(xh, g, slot)

        return action

    def spread_far(group, slot):
        def action(g):
            group.from_far(xh, g, slot)
            group.from_ring(other, g, slot + 1)

        return action

    def finish(g):
        tokens.from_far(other, g, 14)
        tokens.from_core(g)
        compute(g)
        hidden.first(g)

    width = down_ref.shape[1]
    lines = gate_ref.shape[0]

    def compute_out(g):
        deepk = 4 * lines

        def part(k, total):
            left = hid_ref[pl.ds(k * 4, 4), :, columns(g)].reshape(deepk, cols)
            right = down_ref[pl.ds(pl.multiple_of(k * deepk, deepk), deepk), :]
            return total + lax.dot_general(
                left, right, (((0,), (0,)), ((), ())), preferred_element_type=jnp.float32
            )

        out = lax.fori_loop(0, m // 4, part, jnp.zeros((cols, width), jnp.float32))
        for b in range(4):
            for i in range(size):
                for y in range(YS):
                    row = (b * size + i) * tall + y * SLOTS
                    target = fsdp_index(b // 2, y, b % 2)
                    stage[target, g * size + i] = out[row : row + SLOTS].astype(stage.dtype)

    def column_place(g, block):
        return rows.at[
            pl.ds(g * size, size), :, pl.ds(pl.multiple_of(block * width, width), width)
        ]

    def column(g, k, target, origin):
        return pltpu.make_async_remote_copy(
            src_ref=stage.at[target, pl.ds(g * size, size)],
            dst_ref=column_place(g, origin),
            send_sem=c_send.at[g, k],
            recv_sem=c_recv.at[g, k],
            device_id={"fsdp": target},
            device_id_type=MESH,
        )

    def mine(g):
        return pltpu.make_async_copy(
            stage.at[me, pl.ds(g * size, size)], column_place(g, me), mine_sem.at[g]
        )

    def last(g):
        hidden.from_far(other, g, 14)
        hidden.from_core(g)
        compute_out(g)

        def column_start(k, carry):
            column(g, k, lax.rem(me + 1 + k, m), me).start()
            return carry

        lax.fori_loop(0, m - 1, column_start, 0)
        mine(g).start()

    def back(i, target, slot):
        return pltpu.make_async_remote_copy(
            src_ref=rows.at[i],
            dst_ref=y_ref.at[slot],
            send_sem=b_send.at[i],
            recv_sem=b_recv.at[i],
            device_id={"expert": target},
            device_id_type=MESH,
        )

    own_rows = pltpu.make_async_copy(rows.at[n - 1], y_ref.at[e], own_sem.at[1])

    def give_back(g):
        def column_land(k, carry):
            origin = lax.rem(me - 1 - k + m, m)
            column(g, k, origin, origin).wait_recv()
            return carry

        def back_start(i, carry):
            back(i, lax.rem(e - offset_of(i, n) + n, n), e).start()
            return carry

        lax.fori_loop(0, m - 1, column_land, 0)
        mine(g).wait()

        @pl.when(g < PARTS - 1)
        def _():
            lax.fori_loop(g * size, (g + 1) * size, back_start, 0)

        @pl.when(g == PARTS - 1)
        def _():
            lax.fori_loop((PARTS - 1) * size, n - 1, back_start, 0)
            own_rows.start()

    def step(t, carry):
        at_step(t, 0, enter)
        at_step(t, 1, spread_near(tokens, 7))
        at_step(t, 2, spread_far(tokens, 10))
        at_step(t, 3, finish)
        at_step(t, 4, spread_near(hidden, 7))
        at_step(t, 5, spread_far(hidden, 10))
        at_step(t, 6, last)
        at_step(t, 7, give_back)
        return carry

    lax.fori_loop(0, PARTS + 7, step, 0)

    def column_clear(g, carry):
        def one(k, inner):
            column(g, k, lax.rem(me + 1 + k, m), me).wait_send()
            return inner

        return lax.fori_loop(0, m - 1, one, carry)

    def back_finish(i, carry):
        origin = lax.rem(e + offset_of(i, n), n)
        done = back(i, origin, origin)
        done.wait_recv()
        done.wait_send()
        return carry

    lax.fori_loop(0, n - 1, clear, 0)
    lax.fori_loop(0, PARTS, tokens.drain, 0)
    lax.fori_loop(0, PARTS, hidden.drain, 0)
    lax.fori_loop(0, PARTS, column_clear, 0)
    lax.fori_loop(0, n - 1, back_finish, 0)
    own_rows.wait()


def experts_round(x, w_gate, w_up, w_down, n, m, number):
    _, tall, quarter = x.shape
    lines = w_gate.shape[0]
    width = YS * quarter
    vmem = pl.BlockSpec(memory_space=pltpu.VMEM)
    return pl.pallas_call(
        functools.partial(expert_kernel, n, m),
        out_shape=jax.ShapeDtypeStruct((n, SLOTS, width), x.dtype),
        in_specs=[ANY, vmem, vmem, vmem],
        out_specs=ANY,
        scratch_shapes=[
            pltpu.VMEM((4, n * tall, width), x.dtype),
            pltpu.VMEM((m, lines, 4 * n * tall), x.dtype),
            pltpu.VMEM((m, n, SLOTS, width // m), x.dtype),
            pltpu.VMEM((n, SLOTS, width), x.dtype),
            DMA((n - 1,)),
            DMA((n - 1,)),
            DMA((PARTS, 15)),
            DMA((m, PARTS)),
            DMA((PARTS, 15)),
            DMA((m, PARTS)),
            DMA((PARTS, m - 1)),
            DMA((PARTS, m - 1)),
            DMA((n - 1,)),
            DMA((n - 1,)),
            DMA((2,)),
            DMA((PARTS,)),
        ],
        compiler_params=pltpu.CompilerParams(
            collective_id=number, has_side_effects=True, vmem_limit_bytes=8 * VMEM
        ),
    )(x, w_gate, w_up, w_down)


def route(expert_ids, gate_scores, experts):
    weights = gate_scores / jnp.sum(gate_scores, axis=-1, keepdims=True)
    expert_iota = lax.broadcasted_iota(jnp.int32, (1, 1, experts), 2)
    matches = (expert_ids[:, :, None] == expert_iota).astype(jnp.int32)
    chosen = jnp.sum(matches, axis=1, dtype=jnp.int32)
    weight_table = jnp.sum(weights[:, :, None] * matches.astype(jnp.float32), axis=1)
    return chosen, weight_table


def slots_of(chosen):
    ranks = jnp.cumsum(chosen, axis=-2, dtype=jnp.int32) - chosen
    slot_iota = lax.broadcasted_iota(jnp.int32, (1,) * chosen.ndim + (SLOTS,), chosen.ndim)
    return jnp.logical_and(ranks[..., None] == slot_iota, chosen[..., None] > 0)


def on_device(tokens, expert_ids, gate_scores, w_gate, w_up, w_down):
    n_expert = lax.axis_size("expert")
    n_fsdp = lax.axis_size("fsdp")
    local_tok, top_k = expert_ids.shape
    experts = n_expert
    width = tokens.shape[1]
    tall = YS * SLOTS

    chosen, weight_table = route(expert_ids, gate_scores, experts)
    select = jnp.transpose(slots_of(chosen).astype(jnp.float32), (1, 2, 0))
    combine_table = select * jnp.transpose(weight_table)[:, None, :]

    padded = jnp.pad(tokens, ((0, 8 - local_tok), (0, 0)))
    meta = jnp.pad(chosen.astype(jnp.float32), ((0, 8 - local_tok), (0, 128 - experts)))
    tok_quarter, chosen_all = quarters(padded, meta, 0)
    masks = slots_of(chosen_all[:, :, :experts].astype(jnp.int32))
    same = jnp.eye(YS, dtype=jnp.bool_)[None, :, None, :, None]
    table = jnp.transpose(masks, (2, 0, 3, 1))[:, :, :, None, :] & same
    table = table.astype(jnp.bfloat16).reshape(experts * tall, YS * 8)
    outgoing = jnp.dot(
        table, tok_quarter.reshape(YS * 8, width // YS), preferred_element_type=jnp.float32
    )
    outgoing = outgoing.astype(jnp.bfloat16).reshape(experts, tall, width // YS)
    outgoing, combine_table = lax.optimization_barrier((outgoing, combine_table))
    returned = experts_round(
        outgoing, w_gate[0], w_up[0], w_down[0], n_expert, n_fsdp, 1
    )
    mixed = jnp.einsum(
        "ect,ecd->td", combine_table, returned.astype(jnp.float32), precision=lax.Precision.HIGHEST
    )
    return mixed.astype(jnp.bfloat16)


def solution(mesh):
    placed = (
        P(("expert", "fsdp"), None),
        P(("expert", "fsdp"), None),
        P(("expert", "fsdp"), None),
        P("expert", "fsdp", None),
        P("expert", "fsdp", None),
        P("expert", None, "fsdp"),
    )
    return jax.shard_map(
        on_device,
        mesh=mesh,
        in_specs=placed,
        out_specs=P(("expert", "fsdp"), None),
        check_vma=False,
    )
```
